256 devices in a mesh: frame: 16 (over x_hi, z), head: 16 (over y, x_lo, core).
Axes of the slice: x: 4 (x_hi: 2, x_lo: 2; x = x_hi * 2 + x_lo), y: 4, z: 8, core: 2. Of those that a mesh axis runs over, the one named last changes fastest.
Arguments:
- query_proj: bfloat16 [16, 24576, 128], P('head', 'frame'), may hold values from -6 to 6
- key_proj: bfloat16 [16, 24576, 128], P('head', 'frame'), may hold values from -6 to 6
- value_proj: bfloat16 [16, 24576, 128], P('head', 'frame'), may hold values from -6 to 6
- lengths: int32 [32], replicated, may hold values from 384 to 1536, as said below
- out_weight: bfloat16 [1024, 1024], P('head'), may hold values from -0.1875 to 0.1875
Outputs:
- projected: bfloat16 [49152, 1024], P(('frame', 'head'))
The draws below stay inside these ranges and needn't reach their ends.
Inputs may be any that keep to these rules, and one draw needn't show every extreme that they name: `lengths`: some frame has all 1536 tokens valid.
All inputs are finite; a program needn't handle non-finite values.
Results may differ from the reference program's by a relative error of at most 0.0057.
Values may be sent and summed in bfloat16 or wider, within the bound.
A program may use at most 64 MiB of HBM per device.

```python
import math
import jax
import jax.numpy as jnp
from jax import lax

D = 1024
HS = 64
HEADS = 16
FT = 1536
FRAMES = 32
TOKENS = 49152


def rough_normal(key, salt):
    base = jnp.clip(jax.random.normal(jax.random.fold_in(key, salt), (TOKENS, D)), -6.0, 6.0)
    return base


def pack_heads(flat):
    heads_count = D // HS
    return jnp.transpose(flat.reshape(TOKENS, heads_count, HS), (1, 0, 2)).reshape(heads_count, TOKENS // 2, 2 * HS)


def draw_query_proj(key, part):
    base = rough_normal(key, 11)
    return pack_heads(base).astype(jnp.bfloat16)


def draw_key_proj(key, part):
    base = rough_normal(key, 21)
    return pack_heads(base).astype(jnp.bfloat16)


def draw_lengths(key, part):
    counts = jax.random.randint(jax.random.fold_in(key, 3), (FRAMES,), FT // 4, FT + 1)
    full_frame = jax.random.randint(jax.random.fold_in(key, 4), (), 0, FRAMES)
    return jnp.where(jnp.arange(FRAMES) == full_frame, FT, counts).astype(jnp.int32)


def shard_levels(stream_key, dims, cuts, smallest, top_value):
    level, own = 1.0, jax.random.fold_in(stream_key, 6)
    for position, blocks in cuts:
        draws = jnp.exp(jax.random.uniform(jax.random.fold_in(own, position), (blocks,), jnp.float32, smallest / len(cuts), top_value / len(cuts)))
        level = level * jnp.repeat(draws, dims[position] // blocks).reshape([-1 if axis == position else 1 for axis in range(len(dims))])
    return level


def normal_values(rng, extent, scale, reach, split=(), held_as=jnp.bfloat16):
    factor_of = shard_levels(rng, extent, split, -0.22, 0.18) if split else 1.0
    drawn = jax.random.normal(rng, extent, jnp.float32) * scale * factor_of
    return jnp.minimum(jnp.maximum(drawn, -reach), reach).astype(held_as)


def setup_inputs(seed: int = 0) -> dict:
    key_list = jax.random.split(jax.random.key(seed), 6)
    return {
        "query_proj": draw_query_proj(jax.random.fold_in(key_list[5], 71), 0),
        "key_proj": draw_key_proj(jax.random.fold_in(key_list[5], 71), 0),
        "value_proj": normal_values(key_list[2], (HEADS, TOKENS // 2, 2 * HS), 1.0, 6.0, ((0, 16), (1, 16))),
        "lengths": draw_lengths(jax.random.fold_in(key_list[5], 71), 0),
        "out_weight": normal_values(key_list[4], (D, D), D ** -0.5, 0.1875, ((0, 16),)),
    }


def to_grid(packed):
    heads_count = D // HS
    return jnp.transpose(packed.reshape(heads_count, FRAMES, FT, HS), (1, 2, 0, 3))

def reference(query_proj, key_proj, value_proj, lengths, out_weight):
    heads_count = D // HS
    score_scale = 1.0 / math.sqrt(HS)
    strides = (0, 1, 4, 16)
    query_grid = to_grid(query_proj)
    key_grid = to_grid(key_proj)
    value_grid = to_grid(value_proj)
    positions = jnp.arange(FT, dtype=jnp.int32)

    def one_frame(frame_id):
        sources = [(frame_id - stride_len).astype(jnp.int32) for stride_len in strides]
        clipped = [jnp.maximum(source, 0).astype(jnp.int32) for source in sources]
        key_block = jnp.concatenate([lax.dynamic_index_in_dim(key_grid, where_at, 0, keepdims=False) for where_at in clipped], 0)
        value_block = jnp.concatenate([lax.dynamic_index_in_dim(value_grid, where_at, 0, keepdims=False) for where_at in clipped], 0)
        key_valid = jnp.concatenate([(positions < lengths[where_at]) & (source >= 0) for source, where_at in zip(sources, clipped)], 0)
        frame_queries = lax.dynamic_index_in_dim(query_grid, frame_id, 0, keepdims=False)

        def one_head(head_id):
            head_queries = lax.dynamic_index_in_dim(frame_queries, head_id, 1, keepdims=False)
            head_keys = lax.dynamic_index_in_dim(key_block, head_id, 1, keepdims=False)
            head_values = lax.dynamic_index_in_dim(value_block, head_id, 1, keepdims=False)
            scores = jnp.dot(head_queries, head_keys.T, preferred_element_type=jnp.float32) * score_scale
            scores = jnp.where(key_valid[None, :], scores, -jnp.inf)
            top_score = lax.optimization_barrier(jnp.max(scores, axis=1, keepdims=True))
            expon = jnp.where(key_valid[None, :], jnp.exp(scores - top_score), 0.0)
            weights = (expon / lax.optimization_barrier(jnp.sum(expon, axis=1, keepdims=True))).astype(jnp.bfloat16)
            return jnp.dot(weights, head_values, preferred_element_type=jnp.float32).astype(jnp.bfloat16)
        results = lax.map(one_head, jnp.arange(heads_count, dtype=jnp.int32))
        return jnp.transpose(results, (1, 0, 2)).reshape(FT, D)
    attended = lax.map(one_frame, jnp.arange(FRAMES, dtype=jnp.int32)).reshape(TOKENS, D)
    return jnp.dot(attended, out_weight, preferred_element_type=jnp.float32).astype(jnp.bfloat16)
```

```python
import jax
import jax.numpy as jnp
from jax import lax
from jax.experimental import pallas as pl
from jax.experimental.pallas import tpu as pltpu
from jax.sharding import PartitionSpec as P

MESH = pl.DeviceIdType.MESH
BF = jnp.bfloat16
F32 = jnp.float32
HS = 64
PR = 768
KC = 256
NCH = PR // KC
SCALE = 1.4426950408889634 / 8.0
LOW = -1.0e30


def kernel(q_ref, k_ref, v_ref, len_ref, w_ref, o_ref,
           qraw, kprev, vprev, kfar, vfar, qt, ka, vt, s0, s1, m0, m1, acc,
           oout, oin, wbuf, att, abuf, xbuf,
           q_s, q_r, p_s, p_r, f_s, f_r, o_s, o_r, w_s, w_r, g_s, g_r, a_s, a_r):
    d = lax.axis_index("frame")
    h = lax.axis_index("head")
    hp = h // 2
    core = h % 2
    has_prev = d >= 1
    gives_prev = d <= 14
    has_near = d >= 2
    does_near = d <= 13
    has_far = d >= 8

    bar = pltpu.get_barrier_semaphore()
    for shift in (1, 2, 8):
        @pl.when(d >= shift)
        def _():
            pl.semaphore_signal(bar, inc=1, device_id={"frame": d - shift}, device_id_type=MESH)

        @pl.when(d + shift <= 15)
        def _():
            pl.semaphore_signal(bar, inc=1, device_id={"frame": d + shift}, device_id_type=MESH)
    for step in range(1, 16):
        pl.semaphore_signal(bar, inc=1, device_id={"head": (h + step) % 16}, device_id_type=MESH)
    one = lambda c: jnp.where(c, 1, 0)
    pl.semaphore_wait(bar, 16 + one(d >= 1) + one(d <= 14) + one(d >= 2) + one(d <= 13))

    def q_copy(w):
        rows = pl.ds(w * PR, PR)
        return pltpu.make_async_remote_copy(q_ref.at[rows], qraw.at[rows], q_s.at[w], q_r.at[w],
                                            device_id={"frame": d - 2}, device_id_type=MESH)

    def prev_copy(n):
        src, dst = ((k_ref, kprev), (v_ref, vprev))[n]
        return pltpu.make_async_remote_copy(src.at[pl.ds(PR, PR)], dst, p_s.at[n], p_r.at[n],
                                            device_id={"frame": d + 1}, device_id_type=MESH)

    def far_copy(n):
        src, dst = ((k_ref, kfar), (v_ref, vfar))[n]
        return pltpu.make_async_remote_copy(src, dst, f_s.at[n], f_r.at[n],
                                            device_id={"frame": d + 8}, device_id_type=MESH)

    def out_copy(w, par):
        lo, n = ((0, 64), (64, 80))[par]
        return pltpu.make_async_remote_copy(oout.at[w, pl.ds(lo, n)], oin.at[w, pl.ds(lo, n)],
                                            o_s.at[2 * w + par], o_r.at[2 * w + par],
                                            device_id={"frame": d + 2}, device_id_type=MESH)

    def w_rows(head):
        return pl.ds(pl.multiple_of(head * HS, HS), HS)

    def w_copy(step):
        return pltpu.make_async_remote_copy(w_ref, wbuf.at[w_rows(h)], w_s.at[step], w_r.at[hp],
                                            device_id={"head": ((hp + step) % 8) * 2 + core}, device_id_type=MESH)

    def w_wait(step):
        src = (hp + 8 - step) % 8
        return pltpu.make_async_remote_copy(w_ref, wbuf.at[w_rows(2 * src + core)], w_s.at[step], w_r.at[src],
                                            device_id={"head": 2 * src + core}, device_id_type=MESH)

    def g_own():
        return pltpu.make_async_remote_copy(w_ref, wbuf.at[w_rows(h)], g_s.at[hp], g_r.at[hp],
                                            device_id={"head": h + 1 - 2 * core}, device_id_type=MESH)

    def g_copy(step):
        src = (hp + 8 - step) % 8
        rows = w_rows(2 * src + core)
        return pltpu.make_async_remote_copy(wbuf.at[rows], wbuf.at[rows], g_s.at[src], g_r.at[src],
                                            device_id={"head": h + 1 - 2 * core}, device_id_type=MESH)

    def g_wait(src):
        rows = w_rows(2 * src + 1 - core)
        return pltpu.make_async_remote_copy(wbuf.at[rows], wbuf.at[rows], g_s.at[src], g_r.at[src],
                                            device_id={"head": h + 1 - 2 * core}, device_id_type=MESH)

    def a_copy(j):
        return pltpu.make_async_remote_copy(att.at[pl.ds(96 * j, 96)], abuf.at[h], a_s.at[j], a_r.at[h],
                                            device_id={"head": j}, device_id_type=MESH)

    def a_wait(j):
        return pltpu.make_async_remote_copy(att.at[pl.ds(96 * j, 96)], abuf.at[j], a_s.at[j], a_r.at[j],
                                            device_id={"head": j}, device_id_type=MESH)

    @pl.when(has_near)
    def _():
        q_copy(0).start()
        q_copy(1).start()

    @pl.when(gives_prev)
    def _():
        prev_copy(0).start()
        prev_copy(1).start()

    @pl.when(d <= 7)
    def _():
        far_copy(0).start()
        far_copy(1).start()

    for step in range(1, 8):
        w_copy(step).start()
    g_own().start()
    wbuf[w_rows(h), :] = w_ref[...]

    lane = lax.broadcasted_iota(jnp.int32, (PR, 128), 1)
    row = lax.broadcasted_iota(jnp.int32, (PR, 128), 0)
    position = 2 * row + jnp.where(lane >= 64, 1, 0)
    column = lax.broadcasted_iota(jnp.int32, (16, PR), 1)

    def prep_kv(slot, keys, values, frame):
        count = len_ref[jnp.maximum(frame, 0)]
        valid = position < count
        first = jnp.broadcast_to(keys[0:1, :].astype(F32), (PR, 128))
        ka[slot] = jnp.where(valid, keys.astype(F32), first).astype(BF)
        turned = jnp.where(valid, values.astype(F32), 0.0).astype(BF).T
        for p in range(2):
            vt[slot, p, 0:64] = turned[64 * p:64 * p + 64]
            vt[slot, p, 64:80] = jnp.where(2 * column + p < count, 1.0, 0.0).astype(BF)

    def prep_q(slot, queries):
        x = queries.astype(F32) * SCALE
        hi = x.astype(BF)
        low = (x - hi.astype(F32))
        for n, part in enumerate((hi.astype(F32), low)):
            swapped = pltpu.roll(part, 64, 1)
            rows = slice(128 * n, 128 * n + 128)
            qt[slot, 0, 0, rows] = jnp.where(lane < 64, part, 0.0).astype(BF).T
            qt[slot, 0, 1, rows] = jnp.where(lane < 64, 0.0, swapped).astype(BF).T
            qt[slot, 1, 0, rows] = jnp.where(lane < 64, swapped, 0.0).astype(BF).T
            qt[slot, 1, 1, rows] = jnp.where(lane < 64, 0.0, part).astype(BF).T

    for w in range(2):
        prep_q(w, q_ref[pl.ds(w * PR, PR), :])
        prep_kv(w, k_ref[pl.ds(w * PR, PR), :], v_ref[pl.ds(w * PR, PR), :], 2 * d + w)
    for t in range(4):
        for par in range(2):
            acc[t, par, 0:80] = jnp.zeros((80, PR), F32)
            acc[t, par, 80:88] = jnp.full((8, PR), LOW, F32)

    count = jnp.where(has_far, jnp.where(does_near, 8, 6), jnp.where(has_prev, 6, 5))

    def pair_of(i):
        late = jnp.where(i == 3, 4, jnp.where(i == 4, 5, jnp.where(i == 5, 7, i)))
        early = jnp.where(i == 4, jnp.where(has_prev, 4, 6), jnp.where(i == 5, 6, i))
        return jnp.where(does_near, jnp.where(has_far, i, early), late)

    def slots(j):
        q = jnp.where(j == 3, 2, jnp.where(j == 6, 3, jnp.where((j == 1) | (j == 2) | (j == 7), 1, 0)))
        k = jnp.where(j == 4, 2, jnp.where(j == 5, 3, jnp.where(j == 7, 4, jnp.where((j == 1) | (j == 6), 1, 0))))
        return q, k

    chunks = [(c, p) for p in range(2) for c in range(NCH)]

    def score(q, k, par, dst, c, p, top):
        rows = slice((p * NCH + c) * KC, (p * NCH + c + 1) * KC)
        keys = ka[k, c * KC:(c + 1) * KC]
        sc = jnp.dot(jnp.concatenate([keys, keys], axis=1), qt[q, par, p], preferred_element_type=F32)
        dst[rows] = sc
        best = jnp.max(sc.reshape(KC // 8, 8, PR), axis=0)
        return best if top is None else jnp.maximum(top, best)

    def finish_top(top, dst):
        best = jnp.max(top, axis=0, keepdims=True).astype(BF).astype(F32)
        dst[...] = jnp.broadcast_to(best, (8, PR))

    def step(q, k, par, sb, mb, qn, kn, parn, sn, mn):
        m = mb[0:1]
        total, top = None, None
        for c, p in chunks:
            top = score(qn, kn, parn, sn, c, p, top)
            rows = slice((p * NCH + c) * KC, (p * NCH + c + 1) * KC)
            e = jnp.exp2(sb[rows] - m).astype(BF)
            part = jnp.dot(vt[k, p, :, c * KC:(c + 1) * KC], e, preferred_element_type=F32)
            total = part if total is None else total + part
        finish_top(top, mn)
        old = acc[q, par, 80:81]
        new = jnp.maximum(old, m)
        acc[q, par, 0:80] = acc[q, par, 0:80] * jnp.exp2(old - new) + total * jnp.exp2(m - new)
        acc[q, par, 80:88] = jnp.broadcast_to(new, (8, PR))

    def put_near(w, par):
        oout[w, 64 * par:64 * par + 64] = acc[2 + w, par, 0:64].astype(BF)

    def put_stats(w):
        parts = []
        for par in range(2):
            l = acc[2 + w, par, 64:65]
            hi = l.astype(BF).astype(F32)
            parts += [hi, l - hi, acc[2 + w, par, 80:81]]
        pad = jnp.zeros((10, PR), F32)
        oout[w, 128:144] = jnp.concatenate(parts + [pad], axis=0).astype(BF)

    top = None
    for c, p in chunks:
        top = score(0, 0, 0, s0, c, p, top)
    finish_top(top, m0)

    def body(i, _):
        j = pair_of(i)
        nxt = pair_of(jnp.minimum(i + 1, count - 1))
        fresh = i + 1 < count
        for w, at in ((0, 3), (1, 6)):
            @pl.when(fresh & (nxt == at))
            def _():
                q_copy(w).wait_recv()
                prep_q(2 + w, qraw[pl.ds(w * PR, PR), :])

        @pl.when(fresh & (nxt == 4))
        def _():
            prev_copy(0).wait_recv()
            prev_copy(1).wait_recv()
            prep_kv(2, kprev[...], vprev[...], 2 * d - 1)

        @pl.when(fresh & (nxt == 5))
        def _():
            far_copy(0).wait_recv()
            far_copy(1).wait_recv()
            prep_kv(3, kfar[pl.ds(0, PR), :], vfar[pl.ds(0, PR), :], 2 * d - 16)
            prep_kv(4, kfar[pl.ds(PR, PR), :], vfar[pl.ds(PR, PR), :], 2 * d - 15)

        q, k = slots(j)
        qn, kn = slots(nxt)
        step(q, k, 0, s0, m0, q, k, 1, s1, m1)
        for w, at in ((0, 3), (1, 6)):
            @pl.when(j == at)
            def _():
                put_near(w, 0)
                out_copy(w, 0).start()
        step(q, k, 1, s1, m1, qn, kn, 0, s0, m0)
        for w, at in ((0, 3), (1, 6)):
            @pl.when(j == at)
            def _():
                put_near(w, 1)
                put_stats(w)
                out_copy(w, 1).start()

        @pl.when(i == 3)
        def _():
            for s in range(1, 8):
                w_wait(s).wait_recv()
                g_copy(s).start()
        return 0

    lax.fori_loop(0, count, body, 0)

    for w in range(2):
        @pl.when(has_near)
        def _():
            out_copy(w, 0).wait_recv()
            out_copy(w, 1).wait_recv()
            stats = oin[w, 128:144].astype(F32)
            for par in range(2):
                l = stats[3 * par:3 * par + 1] + stats[3 * par + 1:3 * par + 2]
                m = stats[3 * par + 2:3 * par + 3]
                part = oin[w, 64 * par:64 * par + 64].astype(F32)
                old = acc[w, par, 80:81]
                new = jnp.maximum(old, m)
                fo, fn = jnp.exp2(old - new), jnp.exp2(m - new)
                acc[w, par, 0:64] = acc[w, par, 0:64] * fo + part * fn
                acc[w, par, 64:65] = acc[w, par, 64:65] * fo + l * fn
        halves = []
        for par in range(2):
            halves.append((acc[w, par, 0:64] * (1.0 / acc[w, par, 64:65])).astype(BF))
        att[pl.ds(w * PR, PR), :] = jnp.concatenate(halves, axis=0).T
        for j in range(8 * w, 8 * w + 8):
            @pl.when(h == j)
            def _():
                abuf[j] = att[96 * j:96 * j + 96, :]

            @pl.when(h != j)
            def _():
                a_copy(j).start()

    for src in range(8):
        g_wait(src).wait_recv()
    low_half = lax.broadcasted_iota(jnp.int32, (96, 128), 1) < 64
    for n in range(8):
        for j in (2 * n, 2 * n + 1):
            @pl.when(h != j)
            def _():
                a_wait(j).wait_recv()
        a = abuf[2 * n].astype(F32)
        b = abuf[2 * n + 1].astype(F32)
        xbuf[0:96, 128 * n:128 * n + 128] = jnp.where(low_half, a, pltpu.roll(b, 64, 1)).astype(BF)
        xbuf[96:192, 128 * n:128 * n + 128] = jnp.where(low_half, pltpu.roll(a, 64, 1), b).astype(BF)
    out = jnp.dot(xbuf[...], wbuf[...], preferred_element_type=F32).astype(BF)
    o_ref[:, 0:1024] = out[0:96]
    o_ref[:, 1024:2048] = out[96:192]

    @pl.when(has_near)
    def _():
        q_copy(0).wait_send()
        q_copy(1).wait_send()

    @pl.when(gives_prev)
    def _():
        prev_copy(0).wait_send()
        prev_copy(1).wait_send()

    @pl.when(d <= 7)
    def _():
        far_copy(0).wait_send()
        far_copy(1).wait_send()

    @pl.when(does_near)
    def _():
        for w in range(2):
            for par in range(2):
                out_copy(w, par).wait_send()

    g_own().wait_send()
    for s in range(1, 8):
        w_copy(s).wait_send()
        g_copy(s).wait_send()
    for j in range(16):
        @pl.when(h != j)
        def _():
            a_copy(j).wait_send()


def shards(query_proj, key_proj, value_proj, lengths, out_weight):
    vmem = pl.BlockSpec(memory_space=pltpu.VMEM)
    smem = pl.BlockSpec(memory_space=pltpu.SMEM)
    dma = pltpu.SemaphoreType.DMA
    out = pl.pallas_call(
        kernel,
        out_shape=jax.ShapeDtypeStruct((96, 2048), BF),
        in_specs=[vmem, vmem, vmem, smem, vmem],
        out_specs=vmem,
        scratch_shapes=[
            pltpu.VMEM((2 * PR, 128), BF),
            pltpu.VMEM((PR, 128), BF),
            pltpu.VMEM((PR, 128), BF),
            pltpu.VMEM((2 * PR, 128), BF),
            pltpu.VMEM((2 * PR, 128), BF),
            pltpu.VMEM((4, 2, 2, 256, PR), BF),
            pltpu.VMEM((5, PR, 128), BF),
            pltpu.VMEM((5, 2, 80, PR), BF),
            pltpu.VMEM((2 * PR, PR), F32),
            pltpu.VMEM((2 * PR, PR), F32),
            pltpu.VMEM((8, PR), F32),
            pltpu.VMEM((8, PR), F32),
            pltpu.VMEM((4, 2, 88, PR), F32),
            pltpu.VMEM((2, 144, PR), BF),
            pltpu.VMEM((2, 144, PR), BF),
            pltpu.VMEM((1024, 1024), BF),
            pltpu.VMEM((2 * PR, 128), BF),
            pltpu.VMEM((16, 96, 128), BF),
            pltpu.VMEM((192, 1024), BF),
            dma((2,)), dma((2,)), dma((2,)), dma((2,)), dma((2,)), dma((2,)),
            dma((4,)), dma((4,)), dma((8,)), dma((8,)), dma((8,)), dma((8,)),
            dma((16,)), dma((16,)),
        ],
        compiler_params=pltpu.CompilerParams(collective_id=0, has_side_effects=True),
        name="fused",
    )(query_proj[0], key_proj[0], value_proj[0], lengths, out_weight)
    return out.reshape(192, 1024)


def solution(mesh):
    return jax.shard_map(
        shards,
        mesh=mesh,
        in_specs=(
            P("head", "frame", None),
            P("head", "frame", None),
            P("head", "frame", None),
            P(),
            P("head", None),
        ),
        out_specs=P(("frame", "head"), None),
        check_vma=False,
    )
```

```python
import jax
import jax.numpy as jnp
from jax import lax
from jax.experimental import pallas as pl
from jax.experimental.pallas import tpu as pltpu
from jax.sharding import PartitionSpec as P

MESH = pl.DeviceIdType.MESH
BF = jnp.bfloat16
F32 = jnp.float32
HS = 64
PR = 768
KC = 256
NCH = PR // KC
SCALE = 1.4426950408889634 / 8.0
LOW = -1.0e30


def kernel(q_ref, k_ref, v_ref, len_ref, w_ref, o_ref,
           qraw, kprev, vprev, knear, vnear, kfar, vfar, qt, ka, vt, s0, s1, m0, m1, acc,
           oout, oin, wbuf, att, abuf, xbuf,
           q_s, q_r, p_s, p_r, n_s, n_r, f_s, f_r, o_s, o_r, w_s, w_r, g_s, g_r, a_s, a_r):
    d = lax.axis_index("frame")
    h = lax.axis_index("head")
    hp = h // 2
    core = h % 2
    side = hp % 2
    line = hp // 2
    does = (d <= 13, (d <= 7) & (d != 6), d == 0, d == 6)
    gets = (d >= 2, (d >= 8) & (d != 14), d == 8, d == 8)
    away = (2, 8, 8, 2)
    place = (0, 1, 2, 2)
    has_prev = d >= 1
    gives_prev = d <= 14
    has_relay = (d >= 2) & (d != 8)
    gives_relay = (d >= 1) & (d <= 14) & (d != 7)
    has_far = (d >= 9, d == 14)
    gives_far = ((d >= 1) & (d <= 7), d == 6)

    def digits(values):
        return sum(v << (4 * n) for n, v in enumerate(values))

    order = jnp.where(d <= 7, digits((0, 1, 2, 3, 4, 7, 6)), digits((0, 1, 2, 3, 4, 5, 6)))
    order = jnp.where(d == 0, digits((0, 1, 2, 3, 7, 9)), order)
    order = jnp.where(d == 6, digits((0, 1, 2, 3, 9, 4, 6)), order)
    order = jnp.where(d == 14, digits((0, 1, 2, 4, 5, 8, 6)), order)
    order = jnp.where(d == 15, digits((0, 1, 2, 4, 5, 6)), order)
    count = jnp.where((d <= 1) | (d == 15), 6, jnp.where(d == 8, 5, 7))

    bar = pltpu.get_barrier_semaphore()
    for shift in (1, 2, 8):
        @pl.when(d >= shift)
        def _():
            pl.semaphore_signal(bar, inc=1, device_id={"frame": d - shift}, device_id_type=MESH)

        @pl.when(d + shift <= 15)
        def _():
            pl.semaphore_signal(bar, inc=1, device_id={"frame": d + shift}, device_id_type=MESH)
    for step in range(1, 16):
        pl.semaphore_signal(bar, inc=1, device_id={"head": (h + step) % 16}, device_id_type=MESH)
    one = lambda c: jnp.where(c, 1, 0)
    pl.semaphore_wait(bar, 16 + one(d >= 1) + one(d <= 14) + one(d >= 2) + one(d <= 13))

    def q_copy(g):
        return pltpu.make_async_remote_copy(q_ref.at[pl.ds((0, 1, 0, 1)[g] * PR, PR)], qraw.at[place[g]], q_s.at[g], q_r.at[g],
                                            device_id={"frame": d - away[g]}, device_id_type=MESH)

    def prev_copy(n):
        src, dst = ((k_ref, kprev), (v_ref, vprev))[n]
        return pltpu.make_async_remote_copy(src.at[pl.ds(PR, PR)], dst, p_s.at[n], p_r.at[n],
                                            device_id={"frame": d + 1}, device_id_type=MESH)

    def relay_copy(n):
        src, dst = ((kprev, knear), (vprev, vnear))[n]
        return pltpu.make_async_remote_copy(src, dst, n_s.at[n], n_r.at[n],
                                            device_id={"frame": d + 1}, device_id_type=MESH)

    def far_copy(w, n):
        src, dst = ((k_ref, kfar), (v_ref, vfar))[n]
        return pltpu.make_async_remote_copy(src.at[pl.ds(w * PR, PR)], dst.at[w], f_s.at[2 * w + n], f_r.at[2 * w + n],
                                            device_id={"frame": d + 8}, device_id_type=MESH)

    def out_copy(g, par):
        lo, n = ((0, 64), (64, 80))[par]
        return pltpu.make_async_remote_copy(oout.at[place[g], pl.ds(lo, n)], oin.at[g, pl.ds(lo, n)],
                                            o_s.at[2 * g + par], o_r.at[2 * g + par],
                                            device_id={"frame": d + away[g]}, device_id_type=MESH)

    def w_rows(head):
        return pl.ds(pl.multiple_of(head * HS, HS), HS)

    def w_copy(step):
        own = step < 4
        shard = hp if own else 2 * line + 1 - side
        to = 2 * line + 1 - side if step == 0 else 2 * ((line + (step if own else step - 3)) % 4) + side
        rows = w_rows(2 * shard + core)
        return pltpu.make_async_remote_copy(w_ref if own else wbuf.at[rows], wbuf.at[rows], w_s.at[step], w_r.at[shard],
                                            device_id={"head": 2 * to + core}, device_id_type=MESH)

    def shard_of(step):
        return 2 * line + 1 - side if step == 0 else (hp + 2 * step) % 8 if step < 4 else 2 * ((line + step - 3) % 4) + 1 - side

    def w_wait(step):
        src = shard_of(step)
        return pltpu.make_async_remote_copy(w_ref, wbuf.at[w_rows(2 * src + core)], w_s.at[step], w_r.at[src],
                                            device_id={"head": 2 * src + core}, device_id_type=MESH)

    def g_own():
        return pltpu.make_async_remote_copy(w_ref, wbuf.at[w_rows(h)], g_s.at[hp], g_r.at[hp],
                                            device_id={"head": h + 1 - 2 * core}, device_id_type=MESH)

    def g_copy(step):
        src = shard_of(step)
        rows = w_rows(2 * src + core)
        return pltpu.make_async_remote_copy(wbuf.at[rows], wbuf.at[rows], g_s.at[src], g_r.at[src],
                                            device_id={"head": h + 1 - 2 * core}, device_id_type=MESH)

    def g_wait(src):
        rows = w_rows(2 * src + 1 - core)
        return pltpu.make_async_remote_copy(wbuf.at[rows], wbuf.at[rows], g_s.at[src], g_r.at[src],
                                            device_id={"head": h + 1 - 2 * core}, device_id_type=MESH)

    def a_copy(j):
        return pltpu.make_async_remote_copy(att.at[pl.ds(96 * j, 96)], abuf.at[h], a_s.at[j], a_r.at[h],
                                            device_id={"head": j}, device_id_type=MESH)

    def a_wait(j):
        return pltpu.make_async_remote_copy(att.at[pl.ds(96 * j, 96)], abuf.at[j], a_s.at[j], a_r.at[j],
                                            device_id={"head": j}, device_id_type=MESH)

    for step in range(4):
        w_copy(step).start()
    g_own().start()

    for g in range(4):
        @pl.when(gets[g])
        def _():
            q_copy(g).start()

    @pl.when(gives_prev)
    def _():
        prev_copy(0).start()
        prev_copy(1).start()

    for w in range(2):
        @pl.when(gives_far[w])
        def _():
            far_copy(w, 0).start()
            far_copy(w, 1).start()

    wbuf[w_rows(h), :] = w_ref[...]

    lane = lax.broadcasted_iota(jnp.int32, (PR, 128), 1)
    row = lax.broadcasted_iota(jnp.int32, (PR, 128), 0)
    position = 2 * row + jnp.where(lane >= 64, 1, 0)
    column = lax.broadcasted_iota(jnp.int32, (16, PR), 1)

    def prep_kv(slot, keys, values, frame):
        count = len_ref[jnp.maximum(frame, 0)]
        valid = position < count
        first = jnp.broadcast_to(keys[0:1, :].astype(F32), (PR, 128))
        ka[slot] = jnp.where(valid, keys.astype(F32), first).astype(BF)
        turned = jnp.where(valid, values.astype(F32), 0.0).astype(BF).T
        for p in range(2):
            vt[slot, p, 0:64] = turned[64 * p:64 * p + 64]
            vt[slot, p, 64:80] = jnp.where(2 * column + p < count, 1.0, 0.0).astype(BF)

    def prep_q(slot, queries):
        x = queries.astype(F32) * SCALE
        hi = x.astype(BF)
        low = (x - hi.astype(F32))
        for n, part in enumerate((hi.astype(F32), low)):
            swapped = pltpu.roll(part, 64, 1)
            rows = slice(128 * n, 128 * n + 128)
            qt[slot, 0, 0, rows] = jnp.where(lane < 64, part, 0.0).astype(BF).T
            qt[slot, 0, 1, rows] = jnp.where(lane < 64, 0.0, swapped).astype(BF).T
            qt[slot, 1, 0, rows] = jnp.where(lane < 64, swapped, 0.0).astype(BF).T
            qt[slot, 1, 1, rows] = jnp.where(lane < 64, 0.0, part).astype(BF).T

    for w in range(2):
        prep_q(w, q_ref[pl.ds(w * PR, PR), :])
        prep_kv(w, k_ref[pl.ds(w * PR, PR), :], v_ref[pl.ds(w * PR, PR), :], 2 * d + w)
    for t in range(5):
        for par in range(2):
            acc[t, par, 0:80] = jnp.zeros((80, PR), F32)
            acc[t, par, 80:88] = jnp.full((8, PR), LOW, F32)

    def pair_of(i):
        return (order >> (4 * i)) & 15

    query_of = sum(v << (3 * n) for n, v in enumerate((0, 1, 1, 2, 0, 0, 1, 3, 1, 4)))
    key_of = sum(v << (3 * n) for n, v in enumerate((0, 1, 0, 0, 2, 3, 4, 1, 5, 0)))

    def slots(j):
        q = (jnp.int32(query_of) >> (3 * j)) & 7
        k = (jnp.int32(key_of) >> (3 * j)) & 7
        return q, jnp.where((j == 9) & (d == 6), 1, k)

    chunks = [(c, p) for p in range(2) for c in range(NCH)]

    def score(q, k, par, dst, c, p, top):
        rows = slice((p * NCH + c) * KC, (p * NCH + c + 1) * KC)
        keys = ka[k, c * KC:(c + 1) * KC]
        sc = jnp.dot(jnp.concatenate([keys, keys], axis=1), qt[q, par, p], preferred_element_type=F32)
        dst[rows] = sc
        best = jnp.max(sc.reshape(KC // 8, 8, PR), axis=0)
        return best if top is None else jnp.maximum(top, best)

    def finish_top(top, dst):
        best = jnp.max(top, axis=0, keepdims=True).astype(BF).astype(F32)
        dst[...] = jnp.broadcast_to(best, (8, PR))

    def step(q, k, par, sb, mb, qn, kn, parn, sn, mn):
        m = mb[0:1]
        total, top = None, None
        for c, p in chunks:
            top = score(qn, kn, parn, sn, c, p, top)
            rows = slice((p * NCH + c) * KC, (p * NCH + c + 1) * KC)
            e = jnp.exp2(sb[rows] - m).astype(BF)
            part = jnp.dot(vt[k, p, :, c * KC:(c + 1) * KC], e, preferred_element_type=F32)
            total = part if total is None else total + part
        finish_top(top, mn)
        old = acc[q, par, 80:81]
        new = jnp.maximum(old, m)
        acc[q, par, 0:80] = acc[q, par, 0:80] * jnp.exp2(old - new) + total * jnp.exp2(m - new)
        acc[q, par, 80:88] = jnp.broadcast_to(new, (8, PR))

    def put_part(n, par):
        oout[n, 64 * par:64 * par + 64] = acc[2 + n, par, 0:64].astype(BF)

    def put_stats(n):
        parts = []
        for par in range(2):
            l = acc[2 + n, par, 64:65]
            hi = l.astype(BF).astype(F32)
            parts += [hi, l - hi, acc[2 + n, par, 80:81]]
        pad = jnp.zeros((10, PR), F32)
        oout[n, 128:144] = jnp.concatenate(parts + [pad], axis=0).astype(BF)

    def give_part(n, par):
        put_part(n, par)
        if par == 1:
            put_stats(n)
        for g in range(4):
            if place[g] == n:
                @pl.when(does[g])
                def _():
                    out_copy(g, par).start()

    jobs = ((0, 3), (1, 7), (2, 9))

    top = None
    for c, p in chunks:
        top = score(0, 0, 0, s0, c, p, top)
    finish_top(top, m0)

    def body(i, _):
        j = pair_of(i)
        nxt = pair_of(jnp.minimum(i + 1, count - 1))
        fresh = i + 1 < count
        for n in range(2):
            @pl.when((i == n + 1) & has_prev)
            def _():
                prev_copy(n).wait_recv()

                @pl.when(gives_relay)
                def _():
                    relay_copy(n).start()

        for n, at in jobs:
            @pl.when(fresh & (nxt == at))
            def _():
                for g in range(4):
                    if place[g] == n:
                        @pl.when(does[g])
                        def _():
                            q_copy(g).wait_recv()
                prep_q(2 + n, qraw[n])

        @pl.when(fresh & (nxt == 4))
        def _():
            prep_kv(2, kprev[...], vprev[...], 2 * d - 1)

        for w, at in ((0, 5), (1, 8)):
            @pl.when(fresh & (nxt == at))
            def _():
                far_copy(w, 0).wait_recv()
                far_copy(w, 1).wait_recv()
                prep_kv((3, 5)[w], kfar[w], vfar[w], 2 * d - 16 + w)

        @pl.when(fresh & (nxt == 6))
        def _():
            relay_copy(0).wait_recv()
            relay_copy(1).wait_recv()
            prep_kv(4, knear[...], vnear[...], 2 * d - 3)

        q, k = slots(j)
        qn, kn = slots(nxt)
        step(q, k, 0, s0, m0, q, k, 1, s1, m1)
        for n, at in jobs:
            @pl.when(j == at)
            def _():
                give_part(n, 0)
        step(q, k, 1, s1, m1, qn, kn, 0, s0, m0)
        for n, at in jobs:
            @pl.when(j == at)
            def _():
                give_part(n, 1)

        @pl.when(i == 1)
        def _():
            w_wait(0).wait_recv()
            for s in range(4, 7):
                w_copy(s).start()

        @pl.when(i == 3)
        def _():
            for s in range(7):
                if s:
                    w_wait(s).wait_recv()
                g_copy(s).start()
        return 0

    lax.fori_loop(0, count, body, 0)

    for w in (1, 0):
        for g in ((0, 2), (1, 3))[w]:
            @pl.when(gets[g])
            def _():
                out_copy(g, 0).wait_recv()
                out_copy(g, 1).wait_recv()
                stats = oin[g, 128:144].astype(F32)
                for par in range(2):
                    l = stats[3 * par:3 * par + 1] + stats[3 * par + 1:3 * par + 2]
                    m = stats[3 * par + 2:3 * par + 3]
                    part = oin[g, 64 * par:64 * par + 64].astype(F32)
                    old = acc[w, par, 80:81]
                    new = jnp.maximum(old, m)
                    fo, fn = jnp.exp2(old - new), jnp.exp2(m - new)
                    acc[w, par, 0:64] = acc[w, par, 0:64] * fo + part * fn
                    acc[w, par, 64:65] = acc[w, par, 64:65] * fo + l * fn
                    acc[w, par, 80:81] = new
        halves = []
        for par in range(2):
            halves.append((acc[w, par, 0:64] * (1.0 / acc[w, par, 64:65])).astype(BF))
        att[pl.ds(w * PR, PR), :] = jnp.concatenate(halves, axis=0).T
        for j in range(8 * w, 8 * w + 8):
            @pl.when(h == j)
            def _():
                abuf[j] = att[96 * j:96 * j + 96, :]

            @pl.when(h != j)
            def _():
                a_copy(j).start()

    for src in range(8):
        g_wait(src).wait_recv()
    low_half = lax.broadcasted_iota(jnp.int32, (96, 128), 1) < 64
    for n in range(8):
        for j in (2 * n, 2 * n + 1):
            @pl.when(h != j)
            def _():
                a_wait(j).wait_recv()
        a = abuf[2 * n].astype(F32)
        b = abuf[2 * n + 1].astype(F32)
        xbuf[0:96, 128 * n:128 * n + 128] = jnp.where(low_half, a, pltpu.roll(b, 64, 1)).astype(BF)
        xbuf[96:192, 128 * n:128 * n + 128] = jnp.where(low_half, pltpu.roll(a, 64, 1), b).astype(BF)
    out = jnp.dot(xbuf[...], wbuf[...], preferred_element_type=F32).astype(BF)
    o_ref[:, 0:1024] = out[0:96]
    o_ref[:, 1024:2048] = out[96:192]

    for g in range(4):
        @pl.when(gets[g])
        def _():
            q_copy(g).wait_send()

        @pl.when(does[g])
        def _():
            out_copy(g, 0).wait_send()
            out_copy(g, 1).wait_send()

    @pl.when(gives_prev)
    def _():
        prev_copy(0).wait_send()
        prev_copy(1).wait_send()

    @pl.when(gives_relay)
    def _():
        relay_copy(0).wait_send()
        relay_copy(1).wait_send()

    for w in range(2):
        @pl.when(gives_far[w])
        def _():
            far_copy(w, 0).wait_send()
            far_copy(w, 1).wait_send()

    g_own().wait_send()
    for s in range(7):
        w_copy(s).wait_send()
        g_copy(s).wait_send()
    for j in range(16):
        @pl.when(h != j)
        def _():
            a_copy(j).wait_send()


def shards(query_proj, key_proj, value_proj, lengths, out_weight):
    vmem = pl.BlockSpec(memory_space=pltpu.VMEM)
    smem = pl.BlockSpec(memory_space=pltpu.SMEM)
    dma = pltpu.SemaphoreType.DMA
    out = pl.pallas_call(
        kernel,
        out_shape=jax.ShapeDtypeStruct((96, 2048), BF),
        in_specs=[vmem, vmem, vmem, smem, vmem],
        out_specs=vmem,
        scratch_shapes=[
            pltpu.VMEM((3, PR, 128), BF),
            pltpu.VMEM((PR, 128), BF),
            pltpu.VMEM((PR, 128), BF),
            pltpu.VMEM((PR, 128), BF),
            pltpu.VMEM((PR, 128), BF),
            pltpu.VMEM((2, PR, 128), BF),
            pltpu.VMEM((2, PR, 128), BF),
            pltpu.VMEM((5, 2, 2, 256, PR), BF),
            pltpu.VMEM((6, PR, 128), BF),
            pltpu.VMEM((6, 2, 80, PR), BF),
            pltpu.VMEM((2 * PR, PR), F32),
            pltpu.VMEM((2 * PR, PR), F32),
            pltpu.VMEM((8, PR), F32),
            pltpu.VMEM((8, PR), F32),
            pltpu.VMEM((5, 2, 88, PR), F32),
            pltpu.VMEM((3, 144, PR), BF),
            pltpu.VMEM((4, 144, PR), BF),
            pltpu.VMEM((1024, 1024), BF),
            pltpu.VMEM((2 * PR, 128), BF),
            pltpu.VMEM((16, 96, 128), BF),
            pltpu.VMEM((192, 1024), BF),
            dma((4,)), dma((4,)), dma((2,)), dma((2,)), dma((2,)), dma((2,)), dma((4,)), dma((4,)),
            dma((8,)), dma((8,)), dma((8,)), dma((8,)), dma((8,)), dma((8,)),
            dma((16,)), dma((16,)),
        ],
        compiler_params=pltpu.CompilerParams(collective_id=0, has_side_effects=True),
        name="fused",
    )(query_proj[0], key_proj[0], value_proj[0], lengths, out_weight)
    return out.reshape(192, 1024)


def solution(mesh):
    return jax.shard_map(
        shards,
        mesh=mesh,
        in_specs=(
            P("head", "frame", None),
            P("head", "frame", None),
            P("head", "frame", None),
            P(),
            P("head", None),
        ),
        out_specs=P(("frame", "head"), None),
        check_vma=False,
    )
```

```python
import jax
import jax.numpy as jnp
from jax import lax
from jax.experimental import pallas as pl
from jax.experimental.pallas import tpu as pltpu
from jax.sharding import PartitionSpec as P

MESH = pl.DeviceIdType.MESH
BF = jnp.bfloat16
F32 = jnp.float32
HS = 64
PR = 768
KC = 256
NCH = PR // KC
SCALE = 1.4426950408889634 / 8.0
LOW = -1.0e30


def kernel(q_ref, k_ref, v_ref, len_ref, w_ref, o_ref,
           qraw, kprev, vprev, knear, vnear, kpass, vpass, kfar, vfar, qt, ka, vt, s0, s1, m0, m1, acc,
           oout, oin, wbuf, att, abuf, xbuf,
           q_s, q_r, p_s, p_r, n_s, n_r, z_s, z_r, f_s, f_r, o_s, o_r, w_s, w_r, g_s, g_r, a_s, a_r):
    d = lax.axis_index("frame")
    h = lax.axis_index("head")
    hp = h // 2
    core = h % 2
    side = hp % 2
    line = hp // 2
    does = (d <= 13, d <= 7)
    gets = (d >= 2, d >= 8)
    away = (2, 8)
    half = (0, 1)
    has_prev = d >= 1
    gives_prev = d <= 14
    gives_relay = (d >= 1) & (d <= 14) & (d != 7)
    gives_far = d <= 7

    def digits(values):
        return sum(v << (4 * n) for n, v in enumerate(values))

    order = jnp.where(d <= 7, digits((0, 1, 2, 3, 4, 7, 6)), digits((0, 1, 2, 3, 4, 5, 6)))
    order = jnp.where(d == 0, digits((0, 1, 2, 3, 7)), order)
    order = jnp.where(d >= 14, digits((0, 1, 2, 4, 5, 6)), order)
    count = jnp.where(d == 0, 5, jnp.where((d == 1) | (d >= 14), 6, 7))

    bar = pltpu.get_barrier_semaphore()
    for shift in (1, 2, 8):
        @pl.when(d >= shift)
        def _():
            pl.semaphore_signal(bar, inc=1, device_id={"frame": d - shift}, device_id_type=MESH)

        @pl.when(d + shift <= 15)
        def _():
            pl.semaphore_signal(bar, inc=1, device_id={"frame": d + shift}, device_id_type=MESH)
    for step in range(1, 16):
        pl.semaphore_signal(bar, inc=1, device_id={"head": (h + step) % 16}, device_id_type=MESH)
    @pl.when((d == 8) | (d == 15))
    def _():
        pl.semaphore_signal(bar, inc=1, device_id={"frame": jnp.where(d == 8, 15, 8)}, device_id_type=MESH)

    def q_copy(g):
        return pltpu.make_async_remote_copy(q_ref.at[pl.ds(half[g] * PR, PR)], qraw.at[g], q_s.at[g], q_r.at[g],
                                            device_id={"frame": d - away[g]}, device_id_type=MESH)

    def prev_copy(n):
        src, dst = ((k_ref, kprev), (v_ref, vprev))[n]
        return pltpu.make_async_remote_copy(src.at[pl.ds(PR, PR)], dst, p_s.at[n], p_r.at[n],
                                            device_id={"frame": d + 1}, device_id_type=MESH)

    def relay_copy(n):
        src, dst = ((kprev, knear), (vprev, vnear))[n]
        return pltpu.make_async_remote_copy(src, dst, n_s.at[n], n_r.at[n],
                                            device_id={"frame": d + 1}, device_id_type=MESH)

    def pass_copy(n):
        src, dst = ((kprev, kpass), (vprev, vpass))[n]
        return pltpu.make_async_remote_copy(src, dst, z_s.at[n], z_r.at[n],
                                            device_id={"frame": d + 8}, device_id_type=MESH)

    def hand_copy(n):
        src, dst = ((kpass, knear), (vpass, vnear))[n]
        return pltpu.make_async_remote_copy(src, dst, n_s.at[n], n_r.at[n],
                                            device_id={"frame": d - 7}, device_id_type=MESH)

    def far_copy(n):
        src, dst = ((k_ref, kfar), (v_ref, vfar))[n]
        return pltpu.make_async_remote_copy(src.at[pl.ds(0, PR)], dst, f_s.at[n], f_r.at[n],
                                            device_id={"frame": d + 8}, device_id_type=MESH)

    def out_copy(g, par):
        lo, n = ((0, 64), (64, 80))[par]
        return pltpu.make_async_remote_copy(oout.at[g, pl.ds(lo, n)], oin.at[g, pl.ds(lo, n)],
                                            o_s.at[2 * g + par], o_r.at[2 * g + par],
                                            device_id={"frame": d + away[g]}, device_id_type=MESH)

    def w_rows(head):
        return pl.ds(pl.multiple_of(head * HS, HS), HS)

    def w_copy(step):
        own = step < 4
        shard = hp if own else 2 * line + 1 - side
        to = 2 * line + 1 - side if step == 0 else 2 * ((line + (step if own else step - 3)) % 4) + side
        rows = w_rows(2 * shard + core)
        return pltpu.make_async_remote_copy(w_ref if own else wbuf.at[rows], wbuf.at[rows], w_s.at[step], w_r.at[shard],
                                            device_id={"head": 2 * to + core}, device_id_type=MESH)

    def shard_of(step):
        return 2 * line + 1 - side if step == 0 else (hp + 2 * step) % 8 if step < 4 else 2 * ((line + step - 3) % 4) + 1 - side

    def w_wait(step):
        src = shard_of(step)
        return pltpu.make_async_remote_copy(w_ref, wbuf.at[w_rows(2 * src + core)], w_s.at[step], w_r.at[src],
                                            device_id={"head": 2 * src + core}, device_id_type=MESH)

    def g_own():
        return pltpu.make_async_remote_copy(w_ref, wbuf.at[w_rows(h)], g_s.at[hp], g_r.at[hp],
                                            device_id={"head": h + 1 - 2 * core}, device_id_type=MESH)

    def g_copy(step):
        src = shard_of(step)
        rows = w_rows(2 * src + core)
        return pltpu.make_async_remote_copy(wbuf.at[rows], wbuf.at[rows], g_s.at[src], g_r.at[src],
                                            device_id={"head": h + 1 - 2 * core}, device_id_type=MESH)

    def g_wait(src):
        rows = w_rows(2 * src + 1 - core)
        return pltpu.make_async_remote_copy(wbuf.at[rows], wbuf.at[rows], g_s.at[src], g_r.at[src],
                                            device_id={"head": h + 1 - 2 * core}, device_id_type=MESH)

    def peer(w, k):
        return 8 * w + (h + k) % 8

    def a_copy(w, k):
        j = peer(w, k)
        return pltpu.make_async_remote_copy(att.at[pl.ds(pl.multiple_of(96 * j, 32), 96)], abuf.at[h],
                                            a_s.at[8 * w + k], a_r.at[h],
                                            device_id={"head": j}, device_id_type=MESH)

    def a_wait(j):
        return pltpu.make_async_remote_copy(att.at[pl.ds(96 * j, 96)], abuf.at[j], a_s.at[j], a_r.at[j],
                                            device_id={"head": j}, device_id_type=MESH)

    wbuf[w_rows(h), :] = w_ref[...]

    lane = lax.broadcasted_iota(jnp.int32, (PR, 128), 1)
    row = lax.broadcasted_iota(jnp.int32, (PR, 128), 0)
    position = 2 * row + jnp.where(lane >= 64, 1, 0)
    column = lax.broadcasted_iota(jnp.int32, (16, PR), 1)

    def prep_kv(slot, keys, values, frame):
        count = len_ref[jnp.maximum(frame, 0)]
        valid = position < count
        first = jnp.broadcast_to(keys[0:1, :].astype(F32), (PR, 128))
        ka[slot] = jnp.where(valid, keys.astype(F32), first).astype(BF)
        turned = jnp.where(valid, values.astype(F32), 0.0).astype(BF).T
        for p in range(2):
            vt[slot, p, 0:64] = turned[64 * p:64 * p + 64]
            vt[slot, p, 64:80] = jnp.where(2 * column + p < count, 1.0, 0.0).astype(BF)

    def prep_q(slot, queries):
        x = queries.astype(F32) * SCALE
        hi = x.astype(BF)
        low = (x - hi.astype(F32))
        for n, part in enumerate((hi, low.astype(BF))):
            turned = part.T
            for par in range(2):
                rows = turned[64 * par:64 * par + 64]
                for p in range(2):
                    at = 128 * n + 64 * p
                    qt[slot, par, p, at:at + 64] = rows
                    at = 128 * n + 64 - 64 * p
                    qt[slot, par, p, at:at + 64] = jnp.zeros((64, PR), BF)

    for w in range(2):
        prep_q(w, q_ref[pl.ds(w * PR, PR), :])
        prep_kv(w, k_ref[pl.ds(w * PR, PR), :], v_ref[pl.ds(w * PR, PR), :], 2 * d + w)
    for t in range(4):
        for par in range(2):
            acc[t, par, 0:80] = jnp.zeros((80, PR), F32)
            acc[t, par, 80:88] = jnp.full((8, PR), LOW, F32)

    one = lambda c: jnp.where(c, 1, 0)
    pl.semaphore_wait(bar, 16 + one(d >= 1) + one(d <= 14) + one(d >= 2) + one(d <= 13) + one((d == 8) | (d == 15)))
    for step in range(4):
        w_copy(step).start()
    g_own().start()

    for g in range(2):
        @pl.when(gets[g])
        def _():
            q_copy(g).start()

    @pl.when(gives_prev)
    def _():
        prev_copy(0).start()
        prev_copy(1).start()

    @pl.when(gives_far)
    def _():
        far_copy(0).start()
        far_copy(1).start()

    def pair_of(i):
        return (order >> (4 * i)) & 15

    query_of = sum(v << (3 * n) for n, v in enumerate((0, 1, 1, 2, 0, 0, 1, 3)))
    key_of = sum(v << (3 * n) for n, v in enumerate((0, 1, 0, 0, 2, 3, 4, 1)))

    def slots(j):
        q = (jnp.int32(query_of) >> (3 * j)) & 7
        k = (jnp.int32(key_of) >> (3 * j)) & 7
        return q, k

    chunks = [(c, p) for p in range(2) for c in range(NCH)]

    def score(q, k, par, dst, c, p, top):
        rows = slice((p * NCH + c) * KC, (p * NCH + c + 1) * KC)
        keys = ka[k, c * KC:(c + 1) * KC]
        sc = jnp.dot(jnp.concatenate([keys, keys], axis=1), qt[q, par, p], preferred_element_type=F32)
        dst[rows] = sc
        best = jnp.max(sc.reshape(KC // 8, 8, PR), axis=0)
        return best if top is None else jnp.maximum(top, best)

    def finish_top(top, dst):
        best = jnp.max(top, axis=0, keepdims=True).astype(BF).astype(F32)
        dst[...] = jnp.broadcast_to(best, (8, PR))

    def step(q, k, par, sb, mb, qn, kn, parn, sn, mn):
        m = mb[0:1]
        total, top = None, None
        for c, p in chunks:
            top = score(qn, kn, parn, sn, c, p, top)
            rows = slice((p * NCH + c) * KC, (p * NCH + c + 1) * KC)
            e = jnp.exp2(sb[rows] - m).astype(BF)
            part = jnp.dot(vt[k, p, :, c * KC:(c + 1) * KC], e, preferred_element_type=F32)
            total = part if total is None else total + part
        finish_top(top, mn)
        old = acc[q, par, 80:81]
        new = jnp.maximum(old, m)
        acc[q, par, 0:80] = acc[q, par, 0:80] * jnp.exp2(old - new) + total * jnp.exp2(m - new)
        acc[q, par, 80:88] = jnp.broadcast_to(new, (8, PR))

    def put_part(n, par):
        oout[n, 64 * par:64 * par + 64] = acc[2 + n, par, 0:64].astype(BF)

    def put_stats(n):
        parts = []
        for par in range(2):
            l = acc[2 + n, par, 64:65]
            hi = l.astype(BF).astype(F32)
            parts += [hi, l - hi, acc[2 + n, par, 80:81]]
        pad = jnp.zeros((10, PR), F32)
        oout[n, 128:144] = jnp.concatenate(parts + [pad], axis=0).astype(BF)

    def give_part(n, par):
        put_part(n, par)
        if par == 1:
            put_stats(n)
        out_copy(n, par).start()

    jobs = ((0, 3), (1, 7))

    top = None
    for c, p in chunks:
        top = score(0, 0, 0, s0, c, p, top)
    finish_top(top, m0)

    def body(i, _):
        j = pair_of(i)
        nxt = pair_of(jnp.minimum(i + 1, count - 1))
        fresh = i + 1 < count
        for n in range(2):
            @pl.when((i == n + 1) & has_prev)
            def _():
                prev_copy(n).wait_recv()

                @pl.when(gives_relay)
                def _():
                    relay_copy(n).start()

                @pl.when(d == 7)
                def _():
                    pass_copy(n).start()

            @pl.when((i == n + 3) & (d == 15))
            def _():
                pass_copy(n).wait_recv()
                hand_copy(n).start()

        for n, at in jobs:
            @pl.when(fresh & (nxt == at))
            def _():
                q_copy(n).wait_recv()
                prep_q(2 + n, qraw[n])

        @pl.when(fresh & (nxt == 4))
        def _():
            prep_kv(2, kprev[...], vprev[...], 2 * d - 1)

        @pl.when(fresh & (nxt == 5))
        def _():
            far_copy(0).wait_recv()
            far_copy(1).wait_recv()
            prep_kv(3, kfar[...], vfar[...], 2 * d - 16)

        @pl.when(fresh & (nxt == 6))
        def _():
            relay_copy(0).wait_recv()
            relay_copy(1).wait_recv()
            prep_kv(4, knear[...], vnear[...], 2 * d - 3)

        q, k = slots(j)
        qn, kn = slots(nxt)
        step(q, k, 0, s0, m0, q, k, 1, s1, m1)
        for n, at in jobs:
            @pl.when(j == at)
            def _():
                give_part(n, 0)
        step(q, k, 1, s1, m1, qn, kn, 0, s0, m0)
        for n, at in jobs:
            @pl.when(j == at)
            def _():
                give_part(n, 1)

        @pl.when(i == 1)
        def _():
            w_wait(0).wait_recv()
            for s in range(4, 7):
                w_copy(s).start()

        @pl.when(i == 3)
        def _():
            for s in range(7):
                if s:
                    w_wait(s).wait_recv()
                g_copy(s).start()
        return 0

    lax.fori_loop(0, count, body, 0)

    for w in (1, 0):
        for g in (w,):
            @pl.when(gets[g])
            def _():
                out_copy(g, 0).wait_recv()
                out_copy(g, 1).wait_recv()
                stats = oin[g, 128:144].astype(F32)
                for par in range(2):
                    l = stats[3 * par:3 * par + 1] + stats[3 * par + 1:3 * par + 2]
                    m = stats[3 * par + 2:3 * par + 3]
                    part = oin[g, 64 * par:64 * par + 64].astype(F32)
                    old = acc[w, par, 80:81]
                    new = jnp.maximum(old, m)
                    fo, fn = jnp.exp2(old - new), jnp.exp2(m - new)
                    acc[w, par, 0:64] = acc[w, par, 0:64] * fo + part * fn
                    acc[w, par, 64:65] = acc[w, par, 64:65] * fo + l * fn
                    acc[w, par, 80:81] = new
        halves = []
        for par in range(2):
            halves.append((acc[w, par, 0:64] * (1.0 / acc[w, par, 64:65])).astype(BF))
        att[pl.ds(w * PR, PR), :] = jnp.concatenate(halves, axis=0).T
        for k in range(1, 8):
            a_copy(w, k).start()

        @pl.when(h // 8 == w)
        def _():
            abuf[h] = att[pl.ds(pl.multiple_of(96 * h, 32), 96), :]

        @pl.when(h // 8 != w)
        def _():
            a_copy(w, 0).start()

    for src in range(8):
        g_wait(src).wait_recv()
    low_half = lax.broadcasted_iota(jnp.int32, (96, 128), 1) < 64
    total = None
    for part in range(4):
        for n in (2 * part, 2 * part + 1):
            for j in (2 * n, 2 * n + 1):
                @pl.when(h != j)
                def _():
                    a_wait(j).wait_recv()
            a = abuf[2 * n].astype(F32)
            b = abuf[2 * n + 1].astype(F32)
            xbuf[0:96, 128 * n:128 * n + 128] = jnp.where(low_half, a, pltpu.roll(b, 64, 1)).astype(BF)
            xbuf[96:192, 128 * n:128 * n + 128] = jnp.where(low_half, pltpu.roll(a, 64, 1), b).astype(BF)
        some = jnp.dot(xbuf[:, 256 * part:256 * part + 256], wbuf[256 * part:256 * part + 256], preferred_element_type=F32)
        total = some if total is None else total + some
    out = total.astype(BF)
    o_ref[:, 0:1024] = out[0:96]
    o_ref[:, 1024:2048] = out[96:192]

    for g in range(2):
        @pl.when(gets[g])
        def _():
            q_copy(g).wait_send()

        @pl.when(does[g])
        def _():
            out_copy(g, 0).wait_send()
            out_copy(g, 1).wait_send()

    @pl.when(gives_prev)
    def _():
        prev_copy(0).wait_send()
        prev_copy(1).wait_send()

    @pl.when(gives_relay)
    def _():
        relay_copy(0).wait_send()
        relay_copy(1).wait_send()

    @pl.when(d == 7)
    def _():
        pass_copy(0).wait_send()
        pass_copy(1).wait_send()

    @pl.when(d == 15)
    def _():
        hand_copy(0).wait_send()
        hand_copy(1).wait_send()

    @pl.when(gives_far)
    def _():
        far_copy(0).wait_send()
        far_copy(1).wait_send()

    g_own().wait_send()
    for s in range(7):
        w_copy(s).wait_send()
        g_copy(s).wait_send()
    for w in range(2):
        for k in range(1, 8):
            a_copy(w, k).wait_send()

        @pl.when(h // 8 != w)
        def _():
            a_copy(w, 0).wait_send()


def shards(query_proj, key_proj, value_proj, lengths, out_weight):
    vmem = pl.BlockSpec(memory_space=pltpu.VMEM)
    smem = pl.BlockSpec(memory_space=pltpu.SMEM)
    dma = pltpu.SemaphoreType.DMA
    out = pl.pallas_call(
        kernel,
        out_shape=jax.ShapeDtypeStruct((96, 2048), BF),
        in_specs=[vmem, vmem, vmem, smem, vmem],
        out_specs=vmem,
        scratch_shapes=[
            pltpu.VMEM((2, PR, 128), BF),
            pltpu.VMEM((PR, 128), BF),
            pltpu.VMEM((PR, 128), BF),
            pltpu.VMEM((PR, 128), BF),
            pltpu.VMEM((PR, 128), BF),
            pltpu.VMEM((PR, 128), BF),
            pltpu.VMEM((PR, 128), BF),
            pltpu.VMEM((PR, 128), BF),
            pltpu.VMEM((PR, 128), BF),
            pltpu.VMEM((4, 2, 2, 256, PR), BF),
            pltpu.VMEM((5, PR, 128), BF),
            pltpu.VMEM((5, 2, 80, PR), BF),
            pltpu.VMEM((2 * PR, PR), F32),
            pltpu.VMEM((2 * PR, PR), F32),
            pltpu.VMEM((8, PR), F32),
            pltpu.VMEM((8, PR), F32),
            pltpu.VMEM((4, 2, 88, PR), F32),
            pltpu.VMEM((2, 144, PR), BF),
            pltpu.VMEM((2, 144, PR), BF),
            pltpu.VMEM((1024, 1024), BF),
            pltpu.VMEM((2 * PR, 128), BF),
            pltpu.VMEM((16, 96, 128), BF),
            pltpu.VMEM((192, 1024), BF),
            dma((2,)), dma((2,)), dma((2,)), dma((2,)), dma((2,)), dma((2,)), dma((2,)), dma((2,)), dma((2,)), dma((2,)),
            dma((4,)), dma((4,)), dma((8,)), dma((8,)), dma((8,)), dma((8,)),
            dma((16,)), dma((16,)),
        ],
        compiler_params=pltpu.CompilerParams(collective_id=0, has_side_effects=True),
        name="fused",
    )(query_proj[0], key_proj[0], value_proj[0], lengths, out_weight)
    return out.reshape(192, 1024)


def solution(mesh):
    return jax.shard_map(
        shards,
        mesh=mesh,
        in_specs=(
            P("head", "frame", None),
            P("head", "frame", None),
            P("head", "frame", None),
            P(),
            P("head", None),
        ),
        out_specs=P(("frame", "head"), None),
        check_vma=False,
    )
```

```python
import jax
import jax.numpy as jnp
from jax import lax
from jax.experimental import pallas as pl
from jax.experimental.pallas import tpu as pltpu
from jax.sharding import PartitionSpec as P

MESH = pl.DeviceIdType.MESH
BF = jnp.bfloat16
F32 = jnp.float32
HS = 64
PR = 768
KC = 256
NCH = PR // KC
SCALE = 1.4426950408889634 / 8.0
LOW = -1.0e30


def kernel(q_ref, k_ref, v_ref, len_ref, w_ref, o_ref,
           qraw, kprev, vprev, knear, vnear, kpass, vpass, kfar, vfar, qt, ka, vt, s0, s1, m0, m1, acc,
           oout, oin, wbuf, att, abuf, xbuf,
           q_s, q_r, p_s, p_r, n_s, n_r, z_s, z_r, f_s, f_r, o_s, o_r, w_s, w_r, g_s, g_r, a_s, a_r):
    d = lax.axis_index("frame")
    h = lax.axis_index("head")
    hp = h // 2
    core = h % 2
    side = hp % 2
    line = hp // 2
    does = (d <= 13, d <= 7)
    gets = (d >= 2, d >= 8)
    away = (2, 8)
    half = (0, 1)
    has_prev = d >= 1
    gives_prev = d <= 14
    gives_relay = (d >= 1) & (d <= 14) & (d != 7)
    gives_far = d <= 7

    def digits(values):
        return sum(v << (4 * n) for n, v in enumerate(values))

    order = jnp.where(d <= 7, digits((0, 1, 2, 3, 4, 7, 6)), digits((0, 1, 2, 3, 4, 5, 6)))
    order = jnp.where(d == 0, digits((0, 1, 2, 3, 7)), order)
    order = jnp.where(d >= 14, digits((0, 1, 2, 4, 5, 6)), order)
    count = jnp.where(d == 0, 5, jnp.where((d == 1) | (d >= 14), 6, 7))

    bar = pltpu.get_barrier_semaphore()
    for shift in (1, 2, 8):
        @pl.when(d >= shift)
        def _():
            pl.semaphore_signal(bar, inc=1, device_id={"frame": d - shift}, device_id_type=MESH)

        @pl.when(d + shift <= 15)
        def _():
            pl.semaphore_signal(bar, inc=1, device_id={"frame": d + shift}, device_id_type=MESH)
    for step in range(1, 16):
        pl.semaphore_signal(bar, inc=1, device_id={"head": (h + step) % 16}, device_id_type=MESH)
    @pl.when((d == 8) | (d == 15))
    def _():
        pl.semaphore_signal(bar, inc=1, device_id={"frame": jnp.where(d == 8, 15, 8)}, device_id_type=MESH)

    def q_copy(g):
        return pltpu.make_async_remote_copy(q_ref.at[pl.ds(half[g] * PR, PR)], qraw.at[g], q_s.at[g], q_r.at[g],
                                            device_id={"frame": d - away[g]}, device_id_type=MESH)

    def prev_copy(n):
        src, dst = ((k_ref, kprev), (v_ref, vprev))[n]
        return pltpu.make_async_remote_copy(src.at[pl.ds(PR, PR)], dst, p_s.at[n], p_r.at[n],
                                            device_id={"frame": d + 1}, device_id_type=MESH)

    def relay_copy(n):
        src, dst = ((kprev, knear), (vprev, vnear))[n]
        return pltpu.make_async_remote_copy(src, dst, n_s.at[n], n_r.at[n],
                                            device_id={"frame": d + 1}, device_id_type=MESH)

    def pass_copy(n):
        src, dst = ((kprev, kpass), (vprev, vpass))[n]
        return pltpu.make_async_remote_copy(src, dst, z_s.at[n], z_r.at[n],
                                            device_id={"frame": d + 8}, device_id_type=MESH)

    def hand_copy(n):
        src, dst = ((kpass, knear), (vpass, vnear))[n]
        return pltpu.make_async_remote_copy(src, dst, n_s.at[n], n_r.at[n],
                                            device_id={"frame": d - 7}, device_id_type=MESH)

    def far_copy(n):
        src, dst = ((k_ref, kfar), (v_ref, vfar))[n]
        return pltpu.make_async_remote_copy(src.at[pl.ds(0, PR)], dst, f_s.at[n], f_r.at[n],
                                            device_id={"frame": d + 8}, device_id_type=MESH)

    def out_copy(g, par):
        lo, n = ((0, 64), (64, 80))[par]
        return pltpu.make_async_remote_copy(oout.at[g, pl.ds(lo, n)], oin.at[g, pl.ds(lo, n)],
                                            o_s.at[2 * g + par], o_r.at[2 * g + par],
                                            device_id={"frame": d + away[g]}, device_id_type=MESH)

    def w_rows(head):
        return pl.ds(pl.multiple_of(head * HS, HS), HS)

    def w_copy(step):
        own = step < 4
        shard = hp if own else 2 * line + 1 - side
        to = 2 * line + 1 - side if step == 0 else 2 * ((line + (step if own else step - 3)) % 4) + side
        rows = w_rows(2 * shard + core)
        return pltpu.make_async_remote_copy(w_ref if own else wbuf.at[rows], wbuf.at[rows], w_s.at[step], w_r.at[shard],
                                            device_id={"head": 2 * to + core}, device_id_type=MESH)

    def shard_of(step):
        return 2 * line + 1 - side if step == 0 else (hp + 2 * step) % 8 if step < 4 else 2 * ((line + step - 3) % 4) + 1 - side

    def w_wait(step):
        src = shard_of(step)
        return pltpu.make_async_remote_copy(w_ref, wbuf.at[w_rows(2 * src + core)], w_s.at[step], w_r.at[src],
                                            device_id={"head": 2 * src + core}, device_id_type=MESH)

    def g_own():
        return pltpu.make_async_remote_copy(w_ref, wbuf.at[w_rows(h)], g_s.at[hp], g_r.at[hp],
                                            device_id={"head": h + 1 - 2 * core}, device_id_type=MESH)

    def g_copy(step):
        src = shard_of(step)
        rows = w_rows(2 * src + core)
        return pltpu.make_async_remote_copy(wbuf.at[rows], wbuf.at[rows], g_s.at[src], g_r.at[src],
                                            device_id={"head": h + 1 - 2 * core}, device_id_type=MESH)

    def g_wait(src):
        rows = w_rows(2 * src + 1 - core)
        return pltpu.make_async_remote_copy(wbuf.at[rows], wbuf.at[rows], g_s.at[src], g_r.at[src],
                                            device_id={"head": h + 1 - 2 * core}, device_id_type=MESH)

    def peer(w, k):
        return 8 * w + (h + k) % 8

    def a_copy(w, k):
        j = peer(w, k)
        return pltpu.make_async_remote_copy(att.at[pl.ds(pl.multiple_of(96 * j, 32), 96)], abuf.at[h],
                                            a_s.at[8 * w + k], a_r.at[h],
                                            device_id={"head": j}, device_id_type=MESH)

    def a_wait(j):
        return pltpu.make_async_remote_copy(att.at[pl.ds(96 * j, 96)], abuf.at[j], a_s.at[j], a_r.at[j],
                                            device_id={"head": j}, device_id_type=MESH)

    wbuf[w_rows(h), :] = w_ref[...]

    lane = lax.broadcasted_iota(jnp.int32, (PR, 128), 1)
    row = lax.broadcasted_iota(jnp.int32, (PR, 128), 0)
    position = 2 * row + jnp.where(lane >= 64, 1, 0)
    column = lax.broadcasted_iota(jnp.int32, (16, PR), 1)

    def prep_kv(slot, keys, values, frame):
        count = len_ref[jnp.maximum(frame, 0)]
        valid = position < count
        first = jnp.broadcast_to(keys[0:1, :].astype(F32), (PR, 128))
        ka[slot] = jnp.where(valid, keys.astype(F32), first).astype(BF)
        turned = jnp.where(valid, values.astype(F32), 0.0).astype(BF).T
        for p in range(2):
            vt[slot, p, 0:64] = turned[64 * p:64 * p + 64]
            vt[slot, p, 64:80] = jnp.where(2 * column + p < count, 1.0, 0.0).astype(BF)

    def prep_q(slot, queries):
        x = queries.astype(F32) * SCALE
        hi = x.astype(BF)
        low = (x - hi.astype(F32))
        for n, part in enumerate((hi, low.astype(BF))):
            turned = part.T
            for par in range(2):
                rows = turned[64 * par:64 * par + 64]
                for p in range(2):
                    at = 128 * n + 64 * p
                    qt[slot, par, p, at:at + 64] = rows
                    at = 128 * n + 64 - 64 * p
                    qt[slot, par, p, at:at + 64] = jnp.zeros((64, PR), BF)

    for w in range(2):
        prep_q(w, q_ref[pl.ds(w * PR, PR), :])
        prep_kv(w, k_ref[pl.ds(w * PR, PR), :], v_ref[pl.ds(w * PR, PR), :], 2 * d + w)
    for t in range(4):
        for par in range(2):
            acc[t, par, 0:80] = jnp.zeros((80, PR), F32)
            acc[t, par, 80:88] = jnp.full((8, PR), LOW, F32)

    one = lambda c: jnp.where(c, 1, 0)
    pl.semaphore_wait(bar, 16 + one(d >= 1) + one(d <= 14) + one(d >= 2) + one(d <= 13) + one((d == 8) | (d == 15)))
    for step in range(4):
        w_copy(step).start()
    g_own().start()

    for g in range(2):
        @pl.when(gets[g])
        def _():
            q_copy(g).start()

    @pl.when(gives_prev)
    def _():
        prev_copy(0).start()
        prev_copy(1).start()

    @pl.when(gives_far)
    def _():
        far_copy(0).start()
        far_copy(1).start()

    def pair_of(i):
        return (order >> (4 * i)) & 15

    query_of = sum(v << (3 * n) for n, v in enumerate((0, 1, 1, 2, 0, 0, 1, 3)))
    key_of = sum(v << (3 * n) for n, v in enumerate((0, 1, 0, 0, 2, 3, 4, 1)))

    def slots(j):
        q = (jnp.int32(query_of) >> (3 * j)) & 7
        k = (jnp.int32(key_of) >> (3 * j)) & 7
        return q, k

    chunks = [(c, p) for p in range(2) for c in range(NCH)]

    def score(q, k, par, dst, c, p, top):
        rows = slice((p * NCH + c) * KC, (p * NCH + c + 1) * KC)
        keys = ka[k, c * KC:(c + 1) * KC]
        sc = jnp.dot(jnp.concatenate([keys, keys], axis=1), qt[q, par, p], preferred_element_type=F32)
        dst[rows] = sc
        best = jnp.max(sc.reshape(KC // 8, 8, PR), axis=0)
        return best if top is None else jnp.maximum(top, best)

    def finish_top(top, dst):
        best = jnp.max(top, axis=0, keepdims=True).astype(BF).astype(F32)
        dst[...] = jnp.broadcast_to(best, (8, PR))

    def step(q, k, par, sb, mb, qn, kn, parn, sn, mn):
        m = mb[0:1]
        total, top = None, None
        for c, p in chunks:
            top = score(qn, kn, parn, sn, c, p, top)
            rows = slice((p * NCH + c) * KC, (p * NCH + c + 1) * KC)
            e = jnp.exp2(sb[rows] - m).astype(BF)
            part = jnp.dot(vt[k, p, :, c * KC:(c + 1) * KC], e, preferred_element_type=F32)
            total = part if total is None else total + part
        finish_top(top, mn)
        old = acc[q, par, 80:81]
        new = jnp.maximum(old, m)
        acc[q, par, 0:80] = acc[q, par, 0:80] * jnp.exp2(old - new) + total * jnp.exp2(m - new)
        acc[q, par, 80:88] = jnp.broadcast_to(new, (8, PR))

    def put_part(n, par):
        oout[n, 64 * par:64 * par + 64] = acc[2 + n, par, 0:64].astype(BF)

    def put_stats(n):
        parts = []
        for par in range(2):
            l = acc[2 + n, par, 64:65]
            hi = l.astype(BF).astype(F32)
            parts += [hi, l - hi, acc[2 + n, par, 80:81]]
        pad = jnp.zeros((10, PR), F32)
        oout[n, 128:144] = jnp.concatenate(parts + [pad], axis=0).astype(BF)

    def give_part(n, par):
        put_part(n, par)
        if par == 1:
            put_stats(n)
        out_copy(n, par).start()

    jobs = ((0, 3), (1, 7))

    top = None
    for c, p in chunks:
        top = score(0, 0, 0, s0, c, p, top)
    finish_top(top, m0)

    def body(i, _):
        j = pair_of(i)
        nxt = pair_of(jnp.minimum(i + 1, count - 1))
        fresh = i + 1 < count
        for n in range(2):
            @pl.when((i == n + 1) & has_prev)
            def _():
                prev_copy(n).wait_recv()

                @pl.when(gives_relay)
                def _():
                    relay_copy(n).start()

                @pl.when(d == 7)
                def _():
                    pass_copy(n).start()

            @pl.when((i == n + 3) & (d == 15))
            def _():
                pass_copy(n).wait_recv()
                hand_copy(n).start()

        q, k = slots(j)
        qn, kn = slots(nxt)
        step(q, k, 0, s0, m0, q, k, 1, s1, m1)
        for n, at in jobs:
            @pl.when(j == at)
            def _():
                give_part(n, 0)
        for n, at in jobs:
            @pl.when(fresh & (nxt == at))
            def _():
                q_copy(n).wait_recv()
                prep_q(2 + n, qraw[n])

        @pl.when(fresh & (nxt == 4))
        def _():
            prep_kv(2, kprev[...], vprev[...], 2 * d - 1)

        @pl.when(fresh & (nxt == 5))
        def _():
            far_copy(0).wait_recv()
            far_copy(1).wait_recv()
            prep_kv(3, kfar[...], vfar[...], 2 * d - 16)

        @pl.when(fresh & (nxt == 6))
        def _():
            relay_copy(0).wait_recv()
            relay_copy(1).wait_recv()
            prep_kv(4, knear[...], vnear[...], 2 * d - 3)

        step(q, k, 1, s1, m1, qn, kn, 0, s0, m0)
        for n, at in jobs:
            @pl.when(j == at)
            def _():
                give_part(n, 1)

        @pl.when(i == 1)
        def _():
            w_wait(0).wait_recv()
            for s in range(4, 7):
                w_copy(s).start()

        @pl.when(i == 3)
        def _():
            for s in range(7):
                if s:
                    w_wait(s).wait_recv()
                g_copy(s).start()
        return 0

    lax.fori_loop(0, count, body, 0)

    for w in (1, 0):
        for g in (w,):
            @pl.when(gets[g])
            def _():
                out_copy(g, 0).wait_recv()
                out_copy(g, 1).wait_recv()
                stats = oin[g, 128:144].astype(F32)
                for par in range(2):
                    l = stats[3 * par:3 * par + 1] + stats[3 * par + 1:3 * par + 2]
                    m = stats[3 * par + 2:3 * par + 3]
                    part = oin[g, 64 * par:64 * par + 64].astype(F32)
                    old = acc[w, par, 80:81]
                    new = jnp.maximum(old, m)
                    fo, fn = jnp.exp2(old - new), jnp.exp2(m - new)
                    acc[w, par, 0:64] = acc[w, par, 0:64] * fo + part * fn
                    acc[w, par, 64:65] = acc[w, par, 64:65] * fo + l * fn
                    acc[w, par, 80:81] = new
        halves = []
        for par in range(2):
            halves.append((acc[w, par, 0:64] * (1.0 / acc[w, par, 64:65])).astype(BF))
        att[pl.ds(w * PR, PR), :] = jnp.concatenate(halves, axis=0).T
        for k in range(1, 8):
            a_copy(w, k).start()

        @pl.when(h // 8 == w)
        def _():
            abuf[h] = att[pl.ds(pl.multiple_of(96 * h, 32), 96), :]

        @pl.when(h // 8 != w)
        def _():
            a_copy(w, 0).start()

    for src in range(8):
        g_wait(src).wait_recv()
    low_half = lax.broadcasted_iota(jnp.int32, (96, 128), 1) < 64
    total = None
    for part in range(4):
        for n in (2 * part, 2 * part + 1):
            for j in (2 * n, 2 * n + 1):
                @pl.when(h != j)
                def _():
                    a_wait(j).wait_recv()
            a = abuf[2 * n].astype(F32)
            b = abuf[2 * n + 1].astype(F32)
            xbuf[0:96, 128 * n:128 * n + 128] = jnp.where(low_half, a, pltpu.roll(b, 64, 1)).astype(BF)
            xbuf[96:192, 128 * n:128 * n + 128] = jnp.where(low_half, pltpu.roll(a, 64, 1), b).astype(BF)
        some = jnp.dot(xbuf[:, 256 * part:256 * part + 256], wbuf[256 * part:256 * part + 256], preferred_element_type=F32)
        total = some if total is None else total + some
    out = total.astype(BF)
    o_ref[:, 0:1024] = out[0:96]
    o_ref[:, 1024:2048] = out[96:192]

    for g in range(2):
        @pl.when(gets[g])
        def _():
            q_copy(g).wait_send()

        @pl.when(does[g])
        def _():
            out_copy(g, 0).wait_send()
            out_copy(g, 1).wait_send()

    @pl.when(gives_prev)
    def _():
        prev_copy(0).wait_send()
        prev_copy(1).wait_send()

    @pl.when(gives_relay)
    def _():
        relay_copy(0).wait_send()
        relay_copy(1).wait_send()

    @pl.when(d == 7)
    def _():
        pass_copy(0).wait_send()
        pass_copy(1).wait_send()

    @pl.when(d == 15)
    def _():
        hand_copy(0).wait_send()
        hand_copy(1).wait_send()

    @pl.when(gives_far)
    def _():
        far_copy(0).wait_send()
        far_copy(1).wait_send()

    g_own().wait_send()
    for s in range(7):
        w_copy(s).wait_send()
        g_copy(s).wait_send()
    for w in range(2):
        for k in range(1, 8):
            a_copy(w, k).wait_send()

        @pl.when(h // 8 != w)
        def _():
            a_copy(w, 0).wait_send()


def shards(query_proj, key_proj, value_proj, lengths, out_weight):
    vmem = pl.BlockSpec(memory_space=pltpu.VMEM)
    smem = pl.BlockSpec(memory_space=pltpu.SMEM)
    dma = pltpu.SemaphoreType.DMA
    out = pl.pallas_call(
        kernel,
        out_shape=jax.ShapeDtypeStruct((96, 2048), BF),
        in_specs=[vmem, vmem, vmem, smem, vmem],
        out_specs=vmem,
        scratch_shapes=[
            pltpu.VMEM((2, PR, 128), BF),
            pltpu.VMEM((PR, 128), BF),
            pltpu.VMEM((PR, 128), BF),
            pltpu.VMEM((PR, 128), BF),
            pltpu.VMEM((PR, 128), BF),
            pltpu.VMEM((PR, 128), BF),
            pltpu.VMEM((PR, 128), BF),
            pltpu.VMEM((PR, 128), BF),
            pltpu.VMEM((PR, 128), BF),
            pltpu.VMEM((4, 2, 2, 256, PR), BF),
            pltpu.VMEM((5, PR, 128), BF),
            pltpu.VMEM((5, 2, 80, PR), BF),
            pltpu.VMEM((2 * PR, PR), F32),
            pltpu.VMEM((2 * PR, PR), F32),
            pltpu.VMEM((8, PR), F32),
            pltpu.VMEM((8, PR), F32),
            pltpu.VMEM((4, 2, 88, PR), F32),
            pltpu.VMEM((2, 144, PR), BF),
            pltpu.VMEM((2, 144, PR), BF),
            pltpu.VMEM((1024, 1024), BF),
            pltpu.VMEM((2 * PR, 128), BF),
            pltpu.VMEM((16, 96, 128), BF),
            pltpu.VMEM((192, 1024), BF),
            dma((2,)), dma((2,)), dma((2,)), dma((2,)), dma((2,)), dma((2,)), dma((2,)), dma((2,)), dma((2,)), dma((2,)),
            dma((4,)), dma((4,)), dma((8,)), dma((8,)), dma((8,)), dma((8,)),
            dma((16,)), dma((16,)),
        ],
        compiler_params=pltpu.CompilerParams(collective_id=0, has_side_effects=True),
        name="fused",
    )(query_proj[0], key_proj[0], value_proj[0], lengths, out_weight)
    return out.reshape(192, 1024)


def solution(mesh):
    return jax.shard_map(
        shards,
        mesh=mesh,
        in_specs=(
            P("head", "frame", None),
            P("head", "frame", None),
            P("head", "frame", None),
            P(),
            P("head", None),
        ),
        out_specs=P(("frame", "head"), None),
        check_vma=False,
    )
```

```python
import jax
import jax.numpy as jnp
from jax import lax
from jax.experimental import pallas as pl
from jax.experimental.pallas import tpu as pltpu
from jax.sharding import PartitionSpec as P

MESH = pl.DeviceIdType.MESH
BF = jnp.bfloat16
F32 = jnp.float32
HS = 64
PR = 768
KC = 256
NCH = PR // KC
SCALE = 1.4426950408889634 / 8.0
LOW = -1.0e30


def kernel(q_ref, k_ref, v_ref, len_ref, w_ref, o_ref,
           qraw, kprev, vprev, knear, vnear, kpass, vpass, kfar, vfar, qt, ka, vt, s0, s1, m0, m1, acc,
           oout, oin, wbuf, att, abuf, xbuf,
           q_s, q_r, p_s, p_r, n_s, n_r, z_s, z_r, f_s, f_r, o_s, o_r, w_s, w_r, g_s, g_r, a_s, a_r):
    d = lax.axis_index("frame")
    h = lax.axis_index("head")
    hp = h // 2
    core = h % 2
    side = hp % 2
    line = hp // 2
    does = (d <= 13, d <= 7)
    gets = (d >= 2, d >= 8)
    away = (2, 8)
    half = (0, 1)
    has_prev = d >= 1
    gives_prev = d <= 14
    gives_relay = (d >= 1) & (d <= 14) & (d != 7)
    gives_far = d <= 7

    def digits(values):
        return sum(v << (4 * n) for n, v in enumerate(values))

    order = jnp.where(d <= 7, digits((0, 1, 2, 3, 7, 4, 6)), digits((0, 1, 2, 3, 4, 5, 6)))
    order = jnp.where(d == 0, digits((0, 1, 2, 3, 7)), order)
    order = jnp.where(d >= 14, digits((0, 1, 2, 4, 5, 6)), order)
    count = jnp.where(d == 0, 5, jnp.where((d == 1) | (d >= 14), 6, 7))

    bar = pltpu.get_barrier_semaphore()
    for shift in (1, 2, 8):
        @pl.when(d >= shift)
        def _():
            pl.semaphore_signal(bar, inc=1, device_id={"frame": d - shift}, device_id_type=MESH)

        @pl.when(d + shift <= 15)
        def _():
            pl.semaphore_signal(bar, inc=1, device_id={"frame": d + shift}, device_id_type=MESH)
    for step in range(1, 16):
        pl.semaphore_signal(bar, inc=1, device_id={"head": (h + step) % 16}, device_id_type=MESH)
    @pl.when((d == 8) | (d == 15))
    def _():
        pl.semaphore_signal(bar, inc=1, device_id={"frame": jnp.where(d == 8, 15, 8)}, device_id_type=MESH)

    def q_copy(g):
        return pltpu.make_async_remote_copy(q_ref.at[pl.ds(half[g] * PR, PR)], qraw.at[g], q_s.at[g], q_r.at[g],
                                            device_id={"frame": d - away[g]}, device_id_type=MESH)

    def prev_copy(n):
        src, dst = ((k_ref, kprev), (v_ref, vprev))[n]
        return pltpu.make_async_remote_copy(src.at[pl.ds(PR, PR)], dst, p_s.at[n], p_r.at[n],
                                            device_id={"frame": d + 1}, device_id_type=MESH)

    def relay_copy(n):
        src, dst = ((kprev, knear), (vprev, vnear))[n]
        return pltpu.make_async_remote_copy(src, dst, n_s.at[n], n_r.at[n],
                                            device_id={"frame": d + 1}, device_id_type=MESH)

    def pass_copy(n):
        src, dst = ((kprev, kpass), (vprev, vpass))[n]
        return pltpu.make_async_remote_copy(src, dst, z_s.at[n], z_r.at[n],
                                            device_id={"frame": d + 8}, device_id_type=MESH)

    def hand_copy(n):
        src, dst = ((kpass, knear), (vpass, vnear))[n]
        return pltpu.make_async_remote_copy(src, dst, n_s.at[n], n_r.at[n],
                                            device_id={"frame": d - 7}, device_id_type=MESH)

    def far_copy(n):
        src, dst = ((k_ref, kfar), (v_ref, vfar))[n]
        return pltpu.make_async_remote_copy(src.at[pl.ds(0, PR)], dst, f_s.at[n], f_r.at[n],
                                            device_id={"frame": d + 8}, device_id_type=MESH)

    def out_copy(g, par):
        lo, n = ((0, 64), (64, 80))[par]
        return pltpu.make_async_remote_copy(oout.at[g, pl.ds(lo, n)], oin.at[g, pl.ds(lo, n)],
                                            o_s.at[2 * g + par], o_r.at[2 * g + par],
                                            device_id={"frame": d + away[g]}, device_id_type=MESH)

    def w_rows(head):
        return pl.ds(pl.multiple_of(head * HS, HS), HS)

    def w_copy(step):
        own = step < 4
        shard = hp if own else 2 * line + 1 - side
        to = 2 * line + 1 - side if step == 0 else 2 * ((line + (step if own else step - 3)) % 4) + side
        rows = w_rows(2 * shard + core)
        return pltpu.make_async_remote_copy(w_ref if own else wbuf.at[rows], wbuf.at[rows], w_s.at[step], w_r.at[shard],
                                            device_id={"head": 2 * to + core}, device_id_type=MESH)

    def shard_of(step):
        return 2 * line + 1 - side if step == 0 else (hp + 2 * step) % 8 if step < 4 else 2 * ((line + step - 3) % 4) + 1 - side

    def w_wait(step):
        src = shard_of(step)
        return pltpu.make_async_remote_copy(w_ref, wbuf.at[w_rows(2 * src + core)], w_s.at[step], w_r.at[src],
                                            device_id={"head": 2 * src + core}, device_id_type=MESH)

    def g_own():
        return pltpu.make_async_remote_copy(w_ref, wbuf.at[w_rows(h)], g_s.at[hp], g_r.at[hp],
                                            device_id={"head": h + 1 - 2 * core}, device_id_type=MESH)

    def g_copy(step):
        src = shard_of(step)
        rows = w_rows(2 * src + core)
        return pltpu.make_async_remote_copy(wbuf.at[rows], wbuf.at[rows], g_s.at[src], g_r.at[src],
                                            device_id={"head": h + 1 - 2 * core}, device_id_type=MESH)

    def g_wait(src):
        rows = w_rows(2 * src + 1 - core)
        return pltpu.make_async_remote_copy(wbuf.at[rows], wbuf.at[rows], g_s.at[src], g_r.at[src],
                                            device_id={"head": h + 1 - 2 * core}, device_id_type=MESH)

    def peer(w, k):
        return 8 * w + (h + k) % 8

    def a_copy(w, k):
        j = peer(w, k)
        return pltpu.make_async_remote_copy(att.at[pl.ds(pl.multiple_of(96 * j, 32), 96)], abuf.at[h],
                                            a_s.at[8 * w + k], a_r.at[h],
                                            device_id={"head": j}, device_id_type=MESH)

    def a_wait(j):
        return pltpu.make_async_remote_copy(att.at[pl.ds(96 * j, 96)], abuf.at[j], a_s.at[j], a_r.at[j],
                                            device_id={"head": j}, device_id_type=MESH)

    wbuf[w_rows(h), :] = w_ref[...]

    lane = lax.broadcasted_iota(jnp.int32, (PR, 128), 1)
    row = lax.broadcasted_iota(jnp.int32, (PR, 128), 0)
    position = 2 * row + jnp.where(lane >= 64, 1, 0)
    column = lax.broadcasted_iota(jnp.int32, (16, PR), 1)

    def prep_kv(slot, keys, values, frame):
        count = len_ref[jnp.maximum(frame, 0)]
        valid = position < count
        first = jnp.broadcast_to(keys[0:1, :].astype(F32), (PR, 128))
        ka[slot] = jnp.where(valid, keys.astype(F32), first).astype(BF)
        turned = jnp.where(valid, values.astype(F32), 0.0).astype(BF).T
        for p in range(2):
            vt[slot, p, 0:64] = turned[64 * p:64 * p + 64]
            vt[slot, p, 64:80] = jnp.where(2 * column + p < count, 1.0, 0.0).astype(BF)

    def prep_q(slot, queries):
        x = queries.astype(F32) * SCALE
        hi = x.astype(BF)
        low = (x - hi.astype(F32))
        for n, part in enumerate((hi, low.astype(BF))):
            turned = part.T
            for par in range(2):
                rows = turned[64 * par:64 * par + 64]
                for p in range(2):
                    at = 128 * n + 64 * p
                    qt[slot, par, p, at:at + 64] = rows
                    at = 128 * n + 64 - 64 * p
                    qt[slot, par, p, at:at + 64] = jnp.zeros((64, PR), BF)

    for w in range(2):
        prep_q(w, q_ref[pl.ds(w * PR, PR), :])
        prep_kv(w, k_ref[pl.ds(w * PR, PR), :], v_ref[pl.ds(w * PR, PR), :], 2 * d + w)
    for t in range(4):
        for par in range(2):
            acc[t, par, 0:80] = jnp.zeros((80, PR), F32)
            acc[t, par, 80:88] = jnp.full((8, PR), LOW, F32)

    one = lambda c: jnp.where(c, 1, 0)
    pl.semaphore_wait(bar, 16 + one(d >= 1) + one(d <= 14) + one(d >= 2) + one(d <= 13) + one((d == 8) | (d == 15)))
    for step in range(4):
        w_copy(step).start()
    g_own().start()

    for g in range(2):
        @pl.when(gets[g])
        def _():
            q_copy(g).start()

    @pl.when(gives_prev)
    def _():
        prev_copy(0).start()
        prev_copy(1).start()

    @pl.when(gives_far)
    def _():
        far_copy(0).start()
        far_copy(1).start()

    def pair_of(i):
        return (order >> (4 * i)) & 15

    query_of = sum(v << (3 * n) for n, v in enumerate((0, 1, 1, 2, 0, 0, 1, 3)))
    key_of = sum(v << (3 * n) for n, v in enumerate((0, 1, 0, 0, 2, 3, 4, 1)))

    def slots(j):
        q = (jnp.int32(query_of) >> (3 * j)) & 7
        k = (jnp.int32(key_of) >> (3 * j)) & 7
        return q, k

    chunks = [(c, p) for p in range(2) for c in range(NCH)]

    def score(q, k, par, dst, c, p, top):
        rows = slice((p * NCH + c) * KC, (p * NCH + c + 1) * KC)
        keys = ka[k, c * KC:(c + 1) * KC]
        sc = jnp.dot(jnp.concatenate([keys, keys], axis=1), qt[q, par, p], preferred_element_type=F32)
        dst[rows] = sc
        best = jnp.max(sc.reshape(KC // 8, 8, PR), axis=0)
        return best if top is None else jnp.maximum(top, best)

    def finish_top(top, dst):
        best = jnp.max(top, axis=0, keepdims=True).astype(BF).astype(F32)
        dst[...] = jnp.broadcast_to(best, (8, PR))

    def step(q, k, par, sb, mb, qn, kn, parn, sn, mn):
        m = mb[0:1]
        total, top = None, None
        for c, p in chunks:
            top = score(qn, kn, parn, sn, c, p, top)
            rows = slice((p * NCH + c) * KC, (p * NCH + c + 1) * KC)
            e = jnp.exp2(sb[rows] - m).astype(BF)
            part = jnp.dot(vt[k, p, :, c * KC:(c + 1) * KC], e, preferred_element_type=F32)
            total = part if total is None else total + part
        finish_top(top, mn)
        old = acc[q, par, 80:81]
        new = jnp.maximum(old, m)
        acc[q, par, 0:80] = acc[q, par, 0:80] * jnp.exp2(old - new) + total * jnp.exp2(m - new)
        acc[q, par, 80:88] = jnp.broadcast_to(new, (8, PR))

    def put_part(n, par):
        oout[n, 64 * par:64 * par + 64] = acc[2 + n, par, 0:64].astype(BF)

    def put_stats(n):
        parts = []
        for par in range(2):
            l = acc[2 + n, par, 64:65]
            hi = l.astype(BF).astype(F32)
            parts += [hi, l - hi, acc[2 + n, par, 80:81]]
        pad = jnp.zeros((10, PR), F32)
        oout[n, 128:144] = jnp.concatenate(parts + [pad], axis=0).astype(BF)

    def give_part(n, par):
        put_part(n, par)
        if par == 1:
            put_stats(n)
        out_copy(n, par).start()

    jobs = ((0, 3), (1, 7))

    top = None
    for c, p in chunks:
        top = score(0, 0, 0, s0, c, p, top)
    finish_top(top, m0)

    def body(i, _):
        j = pair_of(i)
        nxt = pair_of(jnp.minimum(i + 1, count - 1))
        fresh = i + 1 < count
        for n in range(2):
            @pl.when((i == n + 1) & has_prev)
            def _():
                prev_copy(n).wait_recv()

                @pl.when(gives_relay)
                def _():
                    relay_copy(n).start()

                @pl.when(d == 7)
                def _():
                    pass_copy(n).start()

            @pl.when((i == n + 3) & (d == 15))
            def _():
                pass_copy(n).wait_recv()
                hand_copy(n).start()

        q, k = slots(j)
        qn, kn = slots(nxt)
        step(q, k, 0, s0, m0, q, k, 1, s1, m1)
        for n, at in jobs:
            @pl.when(j == at)
            def _():
                give_part(n, 0)
        for n, at in jobs:
            @pl.when(fresh & (nxt == at))
            def _():
                q_copy(n).wait_recv()
                prep_q(2 + n, qraw[n])

        @pl.when(fresh & (nxt == 4))
        def _():
            prep_kv(2, kprev[...], vprev[...], 2 * d - 1)

        @pl.when(fresh & (nxt == 5))
        def _():
            far_copy(0).wait_recv()
            far_copy(1).wait_recv()
            prep_kv(3, kfar[...], vfar[...], 2 * d - 16)

        @pl.when(fresh & (nxt == 6))
        def _():
            relay_copy(0).wait_recv()
            relay_copy(1).wait_recv()
            prep_kv(4, knear[...], vnear[...], 2 * d - 3)

        step(q, k, 1, s1, m1, qn, kn, 0, s0, m0)
        for n, at in jobs:
            @pl.when(j == at)
            def _():
                give_part(n, 1)

        @pl.when(i == 1)
        def _():
            w_wait(0).wait_recv()
            for s in range(4, 7):
                w_copy(s).start()

        @pl.when(i == 3)
        def _():
            for s in range(7):
                if s:
                    w_wait(s).wait_recv()
                g_copy(s).start()
        return 0

    lax.fori_loop(0, count, body, 0)

    for w in (1, 0):
        for g in (w,):
            @pl.when(gets[g])
            def _():
                out_copy(g, 0).wait_recv()
                out_copy(g, 1).wait_recv()
                stats = oin[g, 128:144].astype(F32)
                for par in range(2):
                    l = stats[3 * par:3 * par + 1] + stats[3 * par + 1:3 * par + 2]
                    m = stats[3 * par + 2:3 * par + 3]
                    part = oin[g, 64 * par:64 * par + 64].astype(F32)
                    old = acc[w, par, 80:81]
                    new = jnp.maximum(old, m)
                    fo, fn = jnp.exp2(old - new), jnp.exp2(m - new)
                    acc[w, par, 0:64] = acc[w, par, 0:64] * fo + part * fn
                    acc[w, par, 64:65] = acc[w, par, 64:65] * fo + l * fn
                    acc[w, par, 80:81] = new
        halves = []
        for par in range(2):
            halves.append((acc[w, par, 0:64] * (1.0 / acc[w, par, 64:65])).astype(BF))
        att[pl.ds(w * PR, PR), :] = jnp.concatenate(halves, axis=0).T
        for k in range(1, 8):
            a_copy(w, k).start()

        @pl.when(h // 8 == w)
        def _():
            abuf[h] = att[pl.ds(pl.multiple_of(96 * h, 32), 96), :]

        @pl.when(h // 8 != w)
        def _():
            a_copy(w, 0).start()

    for src in range(8):
        g_wait(src).wait_recv()
    low_half = lax.broadcasted_iota(jnp.int32, (96, 128), 1) < 64
    total = None
    for part in range(4):
        for n in (2 * part, 2 * part + 1):
            for j in (2 * n, 2 * n + 1):
                @pl.when(h != j)
                def _():
                    a_wait(j).wait_recv()
            a = abuf[2 * n].astype(F32)
            b = abuf[2 * n + 1].astype(F32)
            xbuf[0:96, 128 * n:128 * n + 128] = jnp.where(low_half, a, pltpu.roll(b, 64, 1)).astype(BF)
            xbuf[96:192, 128 * n:128 * n + 128] = jnp.where(low_half, pltpu.roll(a, 64, 1), b).astype(BF)
        some = jnp.dot(xbuf[:, 256 * part:256 * part + 256], wbuf[256 * part:256 * part + 256], preferred_element_type=F32)
        total = some if total is None else total + some
    out = total.astype(BF)
    o_ref[:, 0:1024] = out[0:96]
    o_ref[:, 1024:2048] = out[96:192]

    for g in range(2):
        @pl.when(gets[g])
        def _():
            q_copy(g).wait_send()

        @pl.when(does[g])
        def _():
            out_copy(g, 0).wait_send()
            out_copy(g, 1).wait_send()

    @pl.when(gives_prev)
    def _():
        prev_copy(0).wait_send()
        prev_copy(1).wait_send()

    @pl.when(gives_relay)
    def _():
        relay_copy(0).wait_send()
        relay_copy(1).wait_send()

    @pl.when(d == 7)
    def _():
        pass_copy(0).wait_send()
        pass_copy(1).wait_send()

    @pl.when(d == 15)
    def _():
        hand_copy(0).wait_send()
        hand_copy(1).wait_send()

    @pl.when(gives_far)
    def _():
        far_copy(0).wait_send()
        far_copy(1).wait_send()

    g_own().wait_send()
    for s in range(7):
        w_copy(s).wait_send()
        g_copy(s).wait_send()
    for w in range(2):
        for k in range(1, 8):
            a_copy(w, k).wait_send()

        @pl.when(h // 8 != w)
        def _():
            a_copy(w, 0).wait_send()


def shards(query_proj, key_proj, value_proj, lengths, out_weight):
    vmem = pl.BlockSpec(memory_space=pltpu.VMEM)
    smem = pl.BlockSpec(memory_space=pltpu.SMEM)
    dma = pltpu.SemaphoreType.DMA
    out = pl.pallas_call(
        kernel,
        out_shape=jax.ShapeDtypeStruct((96, 2048), BF),
        in_specs=[vmem, vmem, vmem, smem, vmem],
        out_specs=vmem,
        scratch_shapes=[
            pltpu.VMEM((2, PR, 128), BF),
            pltpu.VMEM((PR, 128), BF),
            pltpu.VMEM((PR, 128), BF),
            pltpu.VMEM((PR, 128), BF),
            pltpu.VMEM((PR, 128), BF),
            pltpu.VMEM((PR, 128), BF),
            pltpu.VMEM((PR, 128), BF),
            pltpu.VMEM((PR, 128), BF),
            pltpu.VMEM((PR, 128), BF),
            pltpu.VMEM((4, 2, 2, 256, PR), BF),
            pltpu.VMEM((5, PR, 128), BF),
            pltpu.VMEM((5, 2, 80, PR), BF),
            pltpu.VMEM((2 * PR, PR), F32),
            pltpu.VMEM((2 * PR, PR), F32),
            pltpu.VMEM((8, PR), F32),
            pltpu.VMEM((8, PR), F32),
            pltpu.VMEM((4, 2, 88, PR), F32),
            pltpu.VMEM((2, 144, PR), BF),
            pltpu.VMEM((2, 144, PR), BF),
            pltpu.VMEM((1024, 1024), BF),
            pltpu.VMEM((2 * PR, 128), BF),
            pltpu.VMEM((16, 96, 128), BF),
            pltpu.VMEM((192, 1024), BF),
            dma((2,)), dma((2,)), dma((2,)), dma((2,)), dma((2,)), dma((2,)), dma((2,)), dma((2,)), dma((2,)), dma((2,)),
            dma((4,)), dma((4,)), dma((8,)), dma((8,)), dma((8,)), dma((8,)),
            dma((16,)), dma((16,)),
        ],
        compiler_params=pltpu.CompilerParams(collective_id=0, has_side_effects=True),
        name="fused",
    )(query_proj[0], key_proj[0], value_proj[0], lengths, out_weight)
    return out.reshape(192, 1024)


def solution(mesh):
    return jax.shard_map(
        shards,
        mesh=mesh,
        in_specs=(
            P("head", "frame", None),
            P("head", "frame", None),
            P("head", "frame", None),
            P(),
            P("head", None),
        ),
        out_specs=P(("frame", "head"), None),
        check_vma=False,
    )
```
